32 devices in a mesh: groups: 2 (over y), row: 4 (over x, core), col: 4 (over z).
Axes of the slice: x: 2, y: 2, z: 4, core: 2. Of those that a mesh axis runs over, the one named last changes fastest.
Arguments:
- queries: bfloat16 [2048, 384], P(('groups', 'row', 'col')), parts along dimension 0, may hold values from -90 to 90
- keys: bfloat16 [2048, 384], P(('groups', 'col', 'row')), parts along dimension 0, may hold values from -15 to 15
- values: bfloat16 [2048, 384], P(('groups', 'col', 'row')), parts along dimension 0, may hold values from -6 to 6
- block_mask: int32 [16, 8], P(('groups', 'row'), 'col'), parts along dimension 0, may hold values from 0 to 1, as said below
- out_weight: bfloat16 [384, 2560], P(None, ('row', 'col')), may hold values from -0.3125 to 0.3125
- residual: bfloat16 [2048, 2560], P(('groups', 'row', 'col')), parts along dimension 0, may hold values from -1.5 to 1.5
Outputs:
- block_out: bfloat16 [2048, 2560], P(('groups', 'row', 'col')), parts along dimension 0
The draws below stay inside these ranges and needn't reach their ends.
There are 2 independent parts, one for each index of `groups`. The reference program is written for one: setup_inputs(seed, part) draws one part's arguments, and reference() takes and returns one part's arrays. A program takes and returns all parts, laid end to end along the dimension named above; an argument that names none is the same for every part. Nothing has to cross between parts.
Inputs may be any that keep to these rules, and one draw needn't show every extreme that they name: Entries are 0 or 1; block_mask[b, b] = 1 for every b. Each query block keeps between 1 and 2 key blocks in each key tile of 2 blocks, and in every pair of a query tile of 2 blocks and a key tile some query block keeps exactly 2.
All inputs are finite; a program needn't handle non-finite values.
Results may differ from the reference program's by a relative error of at most 0.0035.
Values may be sent and summed in bfloat16 or wider, within the bound.
A program may use at most 64 MiB of HBM per device.

```python
import math
import jax
import jax.numpy as jnp
from jax import lax

HD = 128
HEADS = 3
DOUT = 2560
BLK = 128
TOKENS = 1024
NB = 8
QBT = 2
KBT = 2
KEEP_MOST = 2


def paired_fields(key):
    key_query = jax.random.fold_in(key, 11)
    key_key = jax.random.fold_in(key, 12)
    query_field = jnp.clip(jax.random.normal(key_query, (TOKENS, HEADS, HD), jnp.float32), -6.0, 6.0)
    key_field = jnp.clip(2.5 * jax.random.normal(key_key, (TOKENS, HEADS, HD), jnp.float32), -15.0, 15.0)
    return (query_field.reshape(TOKENS, HEADS * HD), key_field.reshape(TOKENS, HEADS * HD))


def draw_queries(key, part):
    query_field, key_field = paired_fields(key)
    return query_field.astype(jnp.bfloat16)


def draw_keys(key, part):
    query_field, key_field = paired_fields(key)
    return key_field.astype(jnp.bfloat16)


def draw_block_mask(key, part):
    tiles = NB // KBT
    first, second, third = jax.random.split(jax.random.fold_in(key, 21), 3)
    within = jnp.arange(KBT, dtype=jnp.int32)
    noise = jax.random.randint(first, (NB, tiles, KBT), 0, 2 ** 20) * KBT + within[None, None, :]
    column = jnp.arange(tiles, dtype=jnp.int32)[None, :, None] * KBT + within[None, None, :]
    row_index = jnp.arange(NB, dtype=jnp.int32)[:, None, None]
    noise = jnp.where(column == row_index, -1, noise)
    ranking = jnp.argsort(jnp.argsort(noise, axis=-1, stable=True), axis=-1, stable=True)
    counts = jax.random.randint(second, (NB, tiles), 1, KEEP_MOST + 1)
    chosen_row = jax.random.randint(third, (NB // QBT, tiles), 0, QBT)
    position = (jnp.arange(NB, dtype=jnp.int32) % QBT)[:, None]
    forced = jnp.repeat(chosen_row, QBT, axis=0)
    counts = jnp.where(position == forced, KEEP_MOST, counts)
    kept = ranking < counts[:, :, None]
    return kept.astype(jnp.int32).reshape(NB, NB)


def steps_of(own_key, extent, shards, smallest, largest):
    loudness, own = 1.0, jax.random.fold_in(own_key, 6)
    for dim, parts in shards:
        draws = jnp.exp(jax.random.uniform(jax.random.fold_in(own, dim), (parts,), jnp.float32, smallest / len(shards), largest / len(shards)))
        loudness = loudness * jnp.repeat(draws, extent[dim] // parts).reshape([-1 if axis == dim else 1 for axis in range(len(extent))])
    return loudness


def normal_values(own_key, extent, spread, bound, cuts=(), kind=jnp.bfloat16):
    loudness = steps_of(own_key, extent, cuts, -0.22, 0.18) if cuts else 1.0
    values = jax.random.normal(own_key, extent, jnp.float32) * spread * loudness
    return jnp.minimum(jnp.maximum(values, -bound), bound).astype(kind)


def setup_inputs(seed: int = 0, part: int = 0) -> dict:
    key_of = jax.random.split(jax.random.key(seed), 7)
    part_splits = jax.random.split(jax.random.fold_in(key_of[6], part), 7)
    return {
        "queries": draw_queries(jax.random.fold_in(jax.random.fold_in(key_of[6], part), 71), part),
        "keys": draw_keys(jax.random.fold_in(jax.random.fold_in(key_of[6], part), 71), part),
        "values": normal_values(part_splits[2], (TOKENS, HEADS * HD), 1.0, 6.0, ((0, 16),)),
        "block_mask": draw_block_mask(jax.random.fold_in(jax.random.fold_in(key_of[6], part), 71), part),
        "out_weight": normal_values(key_of[4], (HEADS * HD, DOUT), (HEADS * HD) ** -0.5, 0.3125, ((1, 16),)),
        "residual": normal_values(part_splits[5], (TOKENS, DOUT), 0.25, 1.5, ((0, 16),)),
    }


def reference(queries, keys, values, block_mask, out_weight, residual):
    score_scale = 1.0 / math.sqrt(HD)
    query_heads = queries.reshape(TOKENS, HEADS, HD)
    key_blocks = keys.reshape(NB, BLK, HEADS, HD)
    value_blocks = values.reshape(NB, BLK, HEADS, HD)
    tiles = NB // KBT
    mask_tiles = block_mask.reshape(NB, tiles, KBT)
    within = jnp.arange(KBT, dtype=jnp.int32)
    tile_start = (jnp.arange(tiles, dtype=jnp.int32) * KBT)[:, None]

    def one_block(index):
        query_rows = lax.dynamic_slice_in_dim(query_heads, (index * BLK).astype(jnp.int32), BLK, 0).astype(jnp.float32)
        mask_row = mask_tiles[index]
        priority = mask_row * (2 * KBT) + (KBT - within)[None, :]
        top_values, chosen = lax.top_k(priority, KEEP_MOST)
        chosen = chosen.astype(jnp.int32)
        usable = jnp.take_along_axis(mask_row, chosen, axis=1) > 0
        picked = (tile_start + chosen).astype(jnp.int32)
        near_keys = key_blocks[picked].astype(jnp.float32)
        near_values = value_blocks[picked].astype(jnp.float32)
        scores = jnp.einsum('qhd,tkbhd->qhtkb', query_rows, near_keys) * score_scale
        scores = jnp.where(usable[None, None, :, :, None], scores, -jnp.inf)
        tile_max = lax.optimization_barrier(jnp.max(scores, axis=(3, 4)))
        weights = jnp.exp(scores - tile_max[:, :, :, None, None])
        tile_total = lax.optimization_barrier(jnp.sum(weights, axis=(3, 4)))
        rounded = lax.optimization_barrier(weights.astype(jnp.bfloat16))
        tile_sum = jnp.einsum('qhtkb,tkbhd->qhtd', rounded.astype(jnp.float32), near_values)
        row_max = lax.optimization_barrier(jnp.max(tile_max, axis=2))
        factor = jnp.exp(tile_max - row_max[:, :, None])
        numer = lax.optimization_barrier(jnp.sum(tile_sum * factor[:, :, :, None], axis=2))
        denom = lax.optimization_barrier(jnp.sum(tile_total * factor, axis=2))
        return (numer / denom[:, :, None]).astype(jnp.bfloat16)
    attended = lax.map(one_block, jnp.arange(NB, dtype=jnp.int32)).reshape(TOKENS, HEADS * HD)
    projected = jnp.dot(attended, out_weight, preferred_element_type=jnp.float32)
    return (projected + residual.astype(jnp.float32)).astype(jnp.bfloat16)
```

```python
import functools
import math

import jax
import jax.numpy as jnp
from jax import lax
from jax.experimental import pallas as pl
from jax.experimental.pallas import tpu as pltpu
from jax.sharding import PartitionSpec as P

HD = 128
HEADS = 3
BLK = 128
MESH = pl.DeviceIdType.MESH


def local(queries, keys, values, block_mask, out_weight, residual):
    score_scale = 1.0 / math.sqrt(HD)
    query_tile = lax.all_gather(queries, "col", axis=0, tiled=True)
    key_tile, value_tile = (
        lax.all_gather(keys, "row", axis=0, tiled=True),
        lax.all_gather(values, "row", axis=0, tiled=True),
    )
    query_count = block_mask.shape[0]
    key_count = block_mask.shape[1]
    keep_most = max(2, 7 * key_count // 16)
    if query_count % 4 == 0:
        group_size = 4
    elif query_count % 2 == 0:
        group_size = 2
    else:
        group_size = 1
    key_blocks = key_tile.reshape(key_count, BLK, HEADS, HD)
    value_blocks = value_tile.reshape(key_count, BLK, HEADS, HD)
    within = jnp.arange(key_count, dtype=jnp.int32)
    priority = block_mask * (2 * key_count) + (key_count - within)[None, :]
    top_values, chosen = lax.top_k(priority, keep_most)
    usable = jnp.take_along_axis(block_mask, chosen, axis=1) > 0
    steps_count = query_count // group_size
    query_groups = query_tile.reshape(steps_count, group_size, BLK, HEADS, HD)
    chosen_groups = chosen.reshape(steps_count, group_size, keep_most)
    usable_groups = usable.reshape(steps_count, group_size, keep_most)

    def one_step(operands):
        query_rows, picked, allowed = operands
        near_keys = key_blocks[picked]
        near_values = value_blocks[picked]
        scores = (
            jnp.einsum(
                "gqhd,gkbhd->gqhkb", query_rows, near_keys, preferred_element_type=jnp.float32
            )
            * score_scale
        )
        scores = jnp.where(allowed[:, None, None, :, None], scores, -jnp.inf)
        tile_max = jnp.max(scores, axis=(3, 4))
        weights = jnp.exp(scores - tile_max[:, :, :, None, None])
        tile_total = jnp.sum(weights, axis=(3, 4))
        rounded = weights.astype(jnp.bfloat16)
        tile_sum = jnp.einsum(
            "gqhkb,gkbhd->gqhd", rounded, near_values, preferred_element_type=jnp.float32
        )
        return (tile_sum, tile_max, tile_total)

    tile_sum, tile_max, tile_total = lax.map(one_step, (query_groups, chosen_groups, usable_groups))
    query_rows_all = query_count * BLK
    tile_sum = tile_sum.reshape(query_rows_all, HEADS, HD)
    tile_max = tile_max.reshape(query_rows_all, HEADS)
    tile_total = tile_total.reshape(query_rows_all, HEADS)
    col_count = lax.axis_size("col")
    own_rows = query_rows_all // col_count
    moved_sum, moved_max, moved_total = (
        lax.all_to_all(
            tile_sum.reshape(col_count, own_rows, HEADS * HD),
            "col",
            split_axis=0,
            concat_axis=0,
            tiled=True,
        ),
        lax.all_to_all(
            tile_max.reshape(col_count, own_rows, HEADS),
            "col",
            split_axis=0,
            concat_axis=0,
            tiled=True,
        ),
        lax.all_to_all(
            tile_total.reshape(col_count, own_rows, HEADS),
            "col",
            split_axis=0,
            concat_axis=0,
            tiled=True,
        ),
    )
    row_max = jnp.max(moved_max, axis=0)
    factor = jnp.exp(moved_max - row_max[None, :, :])
    numer = jnp.sum(
        moved_sum.reshape(col_count, own_rows, HEADS, HD) * factor[:, :, :, None], axis=0
    )
    denom = jnp.sum(moved_total * factor, axis=0)
    attended = (numer / denom[:, :, None]).reshape(own_rows, HEADS * HD).astype(jnp.bfloat16)
    projected = jnp.dot(
        attended,
        lax.all_gather(out_weight, ("row", "col"), axis=1, tiled=True),
        preferred_element_type=jnp.float32,
    )
    return (projected + residual.astype(jnp.float32)).astype(jnp.bfloat16)


def fused_kernel(
    rows, cols, q_in, k_in, v_in, mask_in, w_in, res_in, out_ref,
    qbuf, kv, wt, mask, psend, precv, ssend, srecv,
    osum, res, load_sem, send_sem, recv_sem,
):
    score_scale = 1.0 / math.sqrt(HD)
    g = lax.axis_index("groups")
    r = lax.axis_index("row")
    c = lax.axis_index("col")
    r_chip = lax.rem(r + 2, rows)
    r_core = r + 1 - 2 * lax.rem(r, 2)
    r_both = r_chip + 1 - 2 * lax.rem(r, 2)
    other = 1 - g
    chip = {"row": r_chip}
    core = {"row": r_core}
    video = {"groups": other}
    diagonal = {"groups": other, "row": r_chip}

    loads = [
        pltpu.make_async_copy(q_in, qbuf.at[c], load_sem.at[0]),
        pltpu.make_async_copy(k_in, kv.at[r, 0], load_sem.at[1]),
        pltpu.make_async_copy(v_in, kv.at[r, 1], load_sem.at[2]),
        pltpu.make_async_copy(w_in, wt.at[r, c], load_sem.at[3]),
        pltpu.make_async_copy(mask_in, mask, load_sem.at[4]),
        pltpu.make_async_copy(res_in, res, load_sem.at[5]),
    ]
    for load in loads:
        load.start()

    barrier = pltpu.get_barrier_semaphore()
    peers = [{"col": lax.rem(c + j, cols)} for j in range(1, cols)] + [chip, core, video, diagonal]
    for peer in peers:
        pl.semaphore_signal(barrier, inc=1, device_id=peer, device_id_type=MESH)
    pl.semaphore_wait(barrier, len(peers))

    started = []

    def send(src, dst, device):
        index = len(started)
        copy = pltpu.make_async_remote_copy(
            src_ref=src, dst_ref=dst,
            send_sem=send_sem.at[index], recv_sem=recv_sem.at[index],
            device_id=device, device_id_type=MESH,
        )
        copy.start()
        started.append(copy)
        return copy

    pair = c + 1 - 2 * lax.rem(c, 2)
    across = lax.rem(c + 2, cols)
    far = lax.rem(pair + 2, cols)
    targets = [far, across, pair]
    arriving = []
    to_core = []

    def spread(u, direct=True):
        unit = wt.at[r, u, g]
        if direct:
            arriving.append((wt.at[r_chip, u, other], send(unit, unit, diagonal)))
        arriving.append((wt.at[r_chip, u, g], send(unit, unit, chip)))
        arriving.append((wt.at[r, u, other], send(unit, unit, video)))
        to_core.append(send(unit, unit, core))

    loads[3].wait()
    across_copy = send(wt.at[r, c, g], wt.at[r, c, g], {"col": across})
    pair_copy = send(wt.at[r, c, g], wt.at[r, c, g], {"col": pair})
    loads[0].wait()
    q_copies = [send(qbuf.at[c], qbuf.at[c], {"col": t}) for t in targets]
    loads[1].wait()
    loads[2].wait()
    kv_chip = send(kv.at[r], kv.at[r], chip)
    kv_core = send(kv.at[r], kv.at[r], core)

    half = wt.shape[3]
    own_core = send(wt.at[r, c], wt.at[r, c], core)
    to_core.append(own_core)

    kv_chip.wait_recv()
    kv_both = send(kv.at[r_chip], kv.at[r_chip], core)
    across_copy.wait_recv()
    far_copy = send(wt.at[r, across, g], wt.at[r, across, g], {"col": pair})
    spread(across, direct=False)
    own_chip = send(wt.at[r, c], wt.at[r, c], chip)
    loads[4].wait()
    kv_core.wait_recv()
    kv_both.wait_recv()
    pair_copy.wait_recv()
    spread(pair)
    for copy in q_copies:
        copy.wait_recv()

    own = qbuf.shape[1]
    key_count = mask.shape[1]
    query_count = mask.shape[0]
    for h in range(HEADS):
        lanes = slice(h * HD, (h + 1) * HD)
        key_rows = kv[:, 0, :, lanes].reshape(-1, HD)
        value_rows = kv[:, 1, :, lanes].reshape(-1, HD)
        query_rows = qbuf[:, :, lanes].reshape(-1, HD)
        scores = lax.dot_general(
            key_rows, query_rows, (((1,), (1,)), ((), ())), preferred_element_type=jnp.float32
        )
        scores = scores * score_scale
        seen = jnp.concatenate(
            [
                jnp.concatenate(
                    [
                        jnp.broadcast_to(mask[i : i + 1, j : j + 1], (BLK, BLK))
                        for i in range(query_count)
                    ],
                    axis=1,
                )
                for j in range(key_count)
            ],
            axis=0,
        )
        scores = jnp.where(seen > 0, scores, -jnp.inf)
        tile_max = jnp.max(scores, axis=0, keepdims=True)
        weights = jnp.exp(scores - tile_max)
        tile_total = jnp.sum(weights, axis=0, keepdims=True)
        tile_sum = lax.dot_general(
            weights.astype(jnp.bfloat16), value_rows, (((0,), (0,)), ((), ())),
            preferred_element_type=jnp.float32,
        )
        for i in range(cols):
            part = slice(i * own, (i + 1) * own)
            osum[i, :, lanes] = tile_sum[part]
            psend[i, :, lanes] = tile_sum[part].astype(jnp.bfloat16)
            ssend[i, h : h + 1, 0:own] = tile_max[:, part]
            ssend[i, HEADS + h : HEADS + h + 1, 0:own] = tile_total[:, part]
    p_copies = [send(psend.at[t], precv.at[c], {"col": t}) for t in targets]
    s_copies = [send(ssend.at[t], srecv.at[c], {"col": t}) for t in targets]
    precv[c] = psend[c]
    srecv[c] = ssend[c]

    far_copy.wait_recv()
    spread(far)
    unit, copy = arriving.pop(0)
    copy.wait_recv()
    to_core.append(send(unit, unit, core))
    arriving.append((wt.at[r_chip, across, other], send(unit, unit, video)))
    own_chip.wait_recv()
    to_core.append(send(wt.at[r_chip, c], wt.at[r_chip, c], core))
    for unit, copy in arriving:
        copy.wait_recv()
        to_core.append(send(unit, unit, core))

    for copy in s_copies + p_copies:
        copy.wait_recv()
    stats = [srecv[t] for t in range(cols)]
    maxes = [s[0:HEADS, :] for s in stats]
    totals = [s[HEADS : 2 * HEADS, :] for s in stats]
    row_max = functools.reduce(jnp.maximum, maxes)
    factors = [jnp.exp(m - row_max) for m in maxes]
    denom = functools.reduce(jnp.add, [t * f for t, f in zip(totals, factors)])
    own_factor = jnp.exp(ssend[c, 0:HEADS, :] - row_max)
    low = osum[c] - psend[c].astype(jnp.float32)
    pad = [jnp.zeros((8 - HEADS, denom.shape[1]), jnp.float32)]
    spread = jnp.concatenate(
        [x for f in factors + [denom, own_factor] for x in [f] + pad], axis=0
    )
    fill = jnp.zeros((spread.shape[1] - spread.shape[0], spread.shape[1]), jnp.float32)
    spread = jnp.concatenate([spread, fill], axis=0).T[0:own]
    attended = []
    for h in range(HEADS):
        lanes = slice(h * HD, (h + 1) * HD)
        numer = functools.reduce(
            jnp.add,
            [
                precv[t, :, lanes].astype(jnp.float32) * spread[:, 8 * t + h : 8 * t + h + 1]
                for t in range(cols)
            ],
        )
        numer += low[:, lanes] * spread[:, 8 * cols + 8 + h : 8 * cols + 9 + h]
        attended.append(numer / spread[:, 8 * cols + h : 8 * cols + h + 1])
    attended = jnp.concatenate(attended, axis=1).astype(jnp.bfloat16)

    width = cols * 2 * half

    def project(row):
        columns = pl.ds(pl.multiple_of(row * width, BLK), width)
        projected = lax.dot_general(
            attended, wt[row].reshape(width, HEADS * HD), (((1,), (1,)), ((), ())),
            preferred_element_type=jnp.float32,
        )
        total = projected + res[:, columns].astype(jnp.float32)
        out_ref[:, columns] = total.astype(jnp.bfloat16)

    loads[5].wait()
    project(r)
    project(r_chip)
    for copy in to_core:
        copy.wait_recv()
    project(r_core)
    project(r_both)
    for copy in started:
        copy.wait_send()


def fused(queries, keys, values, block_mask, out_weight, residual):
    rows, cols = lax.axis_size("row"), lax.axis_size("col")
    own, width = queries.shape
    depth, part = out_weight.shape
    copies = 5 * (cols - 1) + 40 + 8 * cols
    any_space = pl.BlockSpec(memory_space=pl.ANY)
    projected = pl.pallas_call(
        functools.partial(fused_kernel, rows, cols),
        out_shape=pltpu.VMEM((own, residual.shape[1]), jnp.bfloat16),
        in_specs=[any_space] * 6,
        out_specs=pl.BlockSpec(memory_space=pltpu.VMEM),
        scratch_shapes=[
            pltpu.VMEM((cols, own, width), jnp.bfloat16),
            pltpu.VMEM((rows, 2, own, width), jnp.bfloat16),
            pltpu.VMEM((rows, cols, 2, part // 2, depth), jnp.bfloat16),
            pltpu.VMEM(block_mask.shape, jnp.int32),
            pltpu.VMEM((cols, own, width), jnp.bfloat16),
            pltpu.VMEM((cols, own, width), jnp.bfloat16),
            pltpu.VMEM((cols, 8, BLK), jnp.float32),
            pltpu.VMEM((cols, 8, BLK), jnp.float32),
            pltpu.VMEM((cols, own, width), jnp.float32),
            pltpu.VMEM(residual.shape, jnp.bfloat16),
            pltpu.SemaphoreType.DMA((6,)),
            pltpu.SemaphoreType.DMA((copies,)),
            pltpu.SemaphoreType.DMA((copies,)),
        ],
        compiler_params=pltpu.CompilerParams(collective_id=0, has_side_effects=True),
    )(queries, keys, values, block_mask, out_weight.T.reshape(2, part // 2, depth), residual)
    return projected


def kernel_fits(mesh):
    return mesh.shape["groups"] == 2 and mesh.shape["row"] == 4 and mesh.shape["col"] == 4


def solution(mesh):
    body = fused if kernel_fits(mesh) else local
    placed = (
        P(("groups", "row", "col"), None),
        P(("groups", "col", "row"), None),
        P(("groups", "col", "row"), None),
        P(("groups", "row"), "col"),
        P(None, ("row", "col")),
        P(("groups", "row", "col"), None),
    )
    return jax.shard_map(
        body,
        mesh=mesh,
        in_specs=placed,
        out_specs=P(("groups", "row", "col"), None),
        check_vma=False,
    )
```

```python
import functools
import math

import jax
import jax.numpy as jnp
from jax import lax
from jax.experimental import pallas as pl
from jax.experimental.pallas import tpu as pltpu
from jax.sharding import PartitionSpec as P

HD = 128
HEADS = 3
BLK = 128
MESH = pl.DeviceIdType.MESH


def local(queries, keys, values, block_mask, out_weight, residual):
    score_scale = 1.0 / math.sqrt(HD)
    query_tile = lax.all_gather(queries, "col", axis=0, tiled=True)
    key_tile, value_tile = (
        lax.all_gather(keys, "row", axis=0, tiled=True),
        lax.all_gather(values, "row", axis=0, tiled=True),
    )
    query_count = block_mask.shape[0]
    key_count = block_mask.shape[1]
    keep_most = max(2, 7 * key_count // 16)
    if query_count % 4 == 0:
        group_size = 4
    elif query_count % 2 == 0:
        group_size = 2
    else:
        group_size = 1
    key_blocks = key_tile.reshape(key_count, BLK, HEADS, HD)
    value_blocks = value_tile.reshape(key_count, BLK, HEADS, HD)
    within = jnp.arange(key_count, dtype=jnp.int32)
    priority = block_mask * (2 * key_count) + (key_count - within)[None, :]
    top_values, chosen = lax.top_k(priority, keep_most)
    usable = jnp.take_along_axis(block_mask, chosen, axis=1) > 0
    steps_count = query_count // group_size
    query_groups = query_tile.reshape(steps_count, group_size, BLK, HEADS, HD)
    chosen_groups = chosen.reshape(steps_count, group_size, keep_most)
    usable_groups = usable.reshape(steps_count, group_size, keep_most)

    def one_step(operands):
        query_rows, picked, allowed = operands
        near_keys = key_blocks[picked]
        near_values = value_blocks[picked]
        scores = (
            jnp.einsum(
                "gqhd,gkbhd->gqhkb", query_rows, near_keys, preferred_element_type=jnp.float32
            )
            * score_scale
        )
        scores = jnp.where(allowed[:, None, None, :, None], scores, -jnp.inf)
        tile_max = jnp.max(scores, axis=(3, 4))
        weights = jnp.exp(scores - tile_max[:, :, :, None, None])
        tile_total = jnp.sum(weights, axis=(3, 4))
        rounded = weights.astype(jnp.bfloat16)
        tile_sum = jnp.einsum(
            "gqhkb,gkbhd->gqhd", rounded, near_values, preferred_element_type=jnp.float32
        )
        return (tile_sum, tile_max, tile_total)

    tile_sum, tile_max, tile_total = lax.map(one_step, (query_groups, chosen_groups, usable_groups))
    query_rows_all = query_count * BLK
    tile_sum = tile_sum.reshape(query_rows_all, HEADS, HD)
    tile_max = tile_max.reshape(query_rows_all, HEADS)
    tile_total = tile_total.reshape(query_rows_all, HEADS)
    col_count = lax.axis_size("col")
    own_rows = query_rows_all // col_count
    moved_sum, moved_max, moved_total = (
        lax.all_to_all(
            tile_sum.reshape(col_count, own_rows, HEADS * HD),
            "col",
            split_axis=0,
            concat_axis=0,
            tiled=True,
        ),
        lax.all_to_all(
            tile_max.reshape(col_count, own_rows, HEADS),
            "col",
            split_axis=0,
            concat_axis=0,
            tiled=True,
        ),
        lax.all_to_all(
            tile_total.reshape(col_count, own_rows, HEADS),
            "col",
            split_axis=0,
            concat_axis=0,
            tiled=True,
        ),
    )
    row_max = jnp.max(moved_max, axis=0)
    factor = jnp.exp(moved_max - row_max[None, :, :])
    numer = jnp.sum(
        moved_sum.reshape(col_count, own_rows, HEADS, HD) * factor[:, :, :, None], axis=0
    )
    denom = jnp.sum(moved_total * factor, axis=0)
    attended = (numer / denom[:, :, None]).reshape(own_rows, HEADS * HD).astype(jnp.bfloat16)
    projected = jnp.dot(
        attended,
        lax.all_gather(out_weight, ("row", "col"), axis=1, tiled=True),
        preferred_element_type=jnp.float32,
    )
    return (projected + residual.astype(jnp.float32)).astype(jnp.bfloat16)


def fused_kernel(
    slots, q_in, k_in, v_in, mask_in, w_in, res_in, out_ref,
    qbuf, kv, wt, mask, psend, precv, ssend, srecv,
    osum, res, blank, load_sem, send_sem, recv_sem,
):
    score_scale = 1.0 / math.sqrt(HD)
    g = lax.axis_index("groups")
    r = lax.axis_index("row")
    c = lax.axis_index("col")
    rows, cols = wt.shape[0], wt.shape[1]
    r_chip = lax.rem(r + 2, rows)
    r_core = r + 1 - 2 * lax.rem(r, 2)
    r_both = r_chip + 1 - 2 * lax.rem(r, 2)
    other = 1 - g
    chip = {"row": r_chip}
    core = {"row": r_core}
    video = {"groups": other}
    diagonal = {"groups": other, "row": r_chip}

    loads = [
        pltpu.make_async_copy(q_in, qbuf.at[c], load_sem.at[0]),
        pltpu.make_async_copy(k_in, kv.at[r, 0], load_sem.at[1]),
        pltpu.make_async_copy(v_in, kv.at[r, 1], load_sem.at[2]),
        pltpu.make_async_copy(w_in, wt.at[r, c], load_sem.at[3]),
        pltpu.make_async_copy(mask_in, mask, load_sem.at[4]),
        pltpu.make_async_copy(res_in, res, load_sem.at[5]),
    ]
    for load in loads:
        load.start()

    barrier = pltpu.get_barrier_semaphore()
    peers = [{"col": lax.rem(c + j, cols)} for j in range(1, cols)] + [chip, core, video, diagonal]
    for peer in peers:
        pl.semaphore_signal(barrier, inc=1, device_id=peer, device_id_type=MESH)
    pl.semaphore_wait(barrier, len(peers))

    bytes_of = {}
    names = []

    def send(src, dst, device, name):
        if name not in bytes_of:
            names.append(name)
            bytes_of[name] = 0
        size = math.prod(dst.shape) * dst.dtype.itemsize
        bytes_of[name] += size
        bytes_of[""] = bytes_of.get("", 0) + size
        pltpu.make_async_remote_copy(
            src_ref=src, dst_ref=dst,
            send_sem=send_sem, recv_sem=recv_sem.at[names.index(name)],
            device_id=device, device_id_type=MESH,
        ).start()

    def settle(sem, size):
        view = blank.at[pl.ds(0, size // (2 * BLK)), :]
        pltpu.make_async_copy(view, view, sem).wait()

    def wait(name):
        settle(recv_sem.at[names.index(name)], bytes_of[name])

    pair = c + 1 - 2 * lax.rem(c, 2)
    across = lax.rem(c + 2, cols)
    far = lax.rem(pair + 2, cols)
    targets = [far, across, pair]

    def spread(u, name, direct=True):
        unit = wt.at[r, u, g]
        if direct:
            send(unit, unit, diagonal, name + "_d")
        send(unit, unit, chip, name + "_x")
        send(unit, unit, video, name + "_y")
        send(unit, unit, core, "core_r")

    def relay_y(u, name):
        wait(name + "_y")
        unit = wt.at[r, u, other]
        send(unit, unit, core, "core_r")

    def relay_x(u, name, forward=False):
        wait(name + "_x")
        unit = wt.at[r_chip, u, g]
        send(unit, unit, core, "core_x")
        if forward:
            send(unit, unit, video, name + "_d")

    def relay_d(u, name):
        wait(name + "_d")
        unit = wt.at[r_chip, u, other]
        send(unit, unit, core, "core_x")

    own = qbuf.shape[1]
    key_count = mask.shape[1]
    query_count = mask.shape[0]
    attended = []

    def attend():
        for h in range(HEADS):
            lanes = slice(h * HD, (h + 1) * HD)
            key_rows = kv[:, 0, :, lanes].reshape(-1, HD)
            value_rows = kv[:, 1, :, lanes].reshape(-1, HD)
            query_rows = qbuf[:, :, lanes].reshape(-1, HD)
            scores = lax.dot_general(
                key_rows, query_rows, (((1,), (1,)), ((), ())), preferred_element_type=jnp.float32
            )
            scores = scores * score_scale
            seen = jnp.concatenate(
                [
                    jnp.concatenate(
                        [
                            jnp.broadcast_to(mask[i : i + 1, j : j + 1], (BLK, BLK))
                            for i in range(query_count)
                        ],
                        axis=1,
                    )
                    for j in range(key_count)
                ],
                axis=0,
            )
            scores = jnp.where(seen > 0, scores, -jnp.inf)
            tile_max = jnp.max(scores, axis=0, keepdims=True)
            weights = jnp.exp(scores - tile_max)
            tile_total = jnp.sum(weights, axis=0, keepdims=True)
            tile_sum = lax.dot_general(
                weights.astype(jnp.bfloat16), value_rows, (((0,), (0,)), ((), ())),
                preferred_element_type=jnp.float32,
            )
            for i in range(cols):
                part = slice(i * own, (i + 1) * own)
                osum[i, :, lanes] = tile_sum[part]
                psend[i, :, lanes] = tile_sum[part].astype(jnp.bfloat16)
                ssend[i, h : h + 1, 0:own] = tile_max[:, part]
                ssend[i, HEADS + h : HEADS + h + 1, 0:own] = tile_total[:, part]
        for t in targets:
            send(ssend.at[t], srecv.at[c], {"col": t}, "p")
            send(psend.at[t], precv.at[c], {"col": t}, "p")
        precv[c] = psend[c]
        srecv[c] = ssend[c]

    def merge():
        wait("p")
        stats = [srecv[t] for t in range(cols)]
        maxes = [s[0:HEADS, :] for s in stats]
        totals = [s[HEADS : 2 * HEADS, :] for s in stats]
        row_max = functools.reduce(jnp.maximum, maxes)
        factors = [jnp.exp(m - row_max) for m in maxes]
        denom = functools.reduce(jnp.add, [t * f for t, f in zip(totals, factors)])
        own_factor = jnp.exp(ssend[c, 0:HEADS, :] - row_max)
        low = osum[c] - psend[c].astype(jnp.float32)
        pad = [jnp.zeros((8 - HEADS, denom.shape[1]), jnp.float32)]
        table = jnp.concatenate(
            [x for f in factors + [denom, own_factor] for x in [f] + pad], axis=0
        )
        fill = jnp.zeros((table.shape[1] - table.shape[0], table.shape[1]), jnp.float32)
        table = jnp.concatenate([table, fill], axis=0).T[0:own]
        heads = []
        for h in range(HEADS):
            lanes = slice(h * HD, (h + 1) * HD)
            numer = functools.reduce(
                jnp.add,
                [
                    precv[t, :, lanes].astype(jnp.float32) * table[:, 8 * t + h : 8 * t + h + 1]
                    for t in range(cols)
                ],
            )
            numer += low[:, lanes] * table[:, 8 * cols + 8 + h : 8 * cols + 9 + h]
            heads.append(numer / table[:, 8 * cols + h : 8 * cols + h + 1])
        attended.append(jnp.concatenate(heads, axis=1).astype(jnp.bfloat16))
        loads[5].wait()

    width = cols * 2 * wt.shape[3]

    def project(row):
        columns = pl.ds(pl.multiple_of(row * width, BLK), width)
        projected = lax.dot_general(
            attended[0], wt[row].reshape(width, HEADS * HD), (((1,), (1,)), ((), ())),
            preferred_element_type=jnp.float32,
        )
        total = projected + res[:, columns].astype(jnp.float32)
        out_ref[:, columns] = total.astype(jnp.bfloat16)

    loads[3].wait()
    send(wt.at[r, c, g], wt.at[r, c, g], {"col": across}, "across")
    send(wt.at[r, c, g], wt.at[r, c, g], {"col": pair}, "pair")
    loads[0].wait()
    for t in targets:
        send(qbuf.at[c], qbuf.at[c], {"col": t}, "q")
    loads[1].wait()
    loads[2].wait()
    send(kv.at[r], kv.at[r], chip, "kv_chip")
    send(kv.at[r], kv.at[r], core, "kv_core")
    send(wt.at[r, c], wt.at[r, c], core, "core_r")
    wait("kv_chip")
    send(kv.at[r_chip], kv.at[r_chip], core, "kv_core")
    wait("across")
    send(wt.at[r, across, g], wt.at[r, across, g], {"col": pair}, "far")
    spread(across, "across", direct=False)
    send(wt.at[r, c], wt.at[r, c], chip, "own_x")
    wait("pair")
    spread(pair, "pair")
    wait("q")
    wait("kv_core")
    loads[4].wait()
    attend()
    wait("far")
    spread(far, "far")
    relay_x(across, "across", forward=True)
    wait("own_x")
    send(wt.at[r_chip, c], wt.at[r_chip, c], core, "core_x")
    relay_y(across, "across")
    relay_x(pair, "pair")
    relay_y(pair, "pair")
    relay_d(pair, "pair")
    relay_x(far, "far")
    relay_y(far, "far")
    relay_d(far, "far")
    relay_d(across, "across")
    merge()
    project(r)
    project(r_chip)
    wait("core_r")
    project(r_core)
    wait("core_x")
    project(r_both)
    assert len(names) == slots, len(names)
    settle(send_sem, bytes_of[""])


def fused(queries, keys, values, block_mask, out_weight, residual):
    rows, cols = lax.axis_size("row"), lax.axis_size("col")
    own, width = queries.shape
    depth, part = out_weight.shape
    slots = 19
    any_space = pl.BlockSpec(memory_space=pl.ANY)
    return pl.pallas_call(
        functools.partial(fused_kernel, slots),
        out_shape=pltpu.VMEM((own, residual.shape[1]), jnp.bfloat16),
        in_specs=[any_space] * 6,
        out_specs=pl.BlockSpec(memory_space=pltpu.VMEM),
        scratch_shapes=[
            pltpu.VMEM((cols, own, width), jnp.bfloat16),
            pltpu.VMEM((rows, 2, own, width), jnp.bfloat16),
            pltpu.VMEM((rows, cols, 2, part // 2, depth), jnp.bfloat16),
            pltpu.VMEM(block_mask.shape, jnp.int32),
            pltpu.VMEM((cols, own, width), jnp.bfloat16),
            pltpu.VMEM((cols, own, width), jnp.bfloat16),
            pltpu.VMEM((cols, 8, BLK), jnp.float32),
            pltpu.VMEM((cols, 8, BLK), jnp.float32),
            pltpu.VMEM((cols, own, width), jnp.float32),
            pltpu.VMEM(residual.shape, jnp.bfloat16),
            pltpu.VMEM((rows * cols * 2 * part * depth // BLK, BLK), jnp.bfloat16),
            pltpu.SemaphoreType.DMA((6,)),
            pltpu.SemaphoreType.DMA,
            pltpu.SemaphoreType.DMA((slots,)),
        ],
        compiler_params=pltpu.CompilerParams(collective_id=0, has_side_effects=True),
    )(queries, keys, values, block_mask, out_weight.T.reshape(2, part // 2, depth), residual)


def kernel_fits(mesh):
    return mesh.shape["groups"] == 2 and mesh.shape["row"] == 4 and mesh.shape["col"] == 4


def solution(mesh):
    body = fused if kernel_fits(mesh) else local
    placed = (
        P(("groups", "row", "col"), None),
        P(("groups", "col", "row"), None),
        P(("groups", "col", "row"), None),
        P(("groups", "row"), "col"),
        P(None, ("row", "col")),
        P(("groups", "row", "col"), None),
    )
    return jax.shard_map(
        body,
        mesh=mesh,
        in_specs=placed,
        out_specs=P(("groups", "row", "col"), None),
        check_vma=False,
    )
```

```python
import functools
import math

import jax
import jax.numpy as jnp
from jax import lax
from jax.experimental import pallas as pl
from jax.experimental.pallas import tpu as pltpu
from jax.sharding import PartitionSpec as P

HD = 128
HEADS = 3
BLK = 128
MESH = pl.DeviceIdType.MESH


def local(queries, keys, values, block_mask, out_weight, residual):
    score_scale = 1.0 / math.sqrt(HD)
    query_tile = lax.all_gather(queries, "col", axis=0, tiled=True)
    key_tile, value_tile = (
        lax.all_gather(keys, "row", axis=0, tiled=True),
        lax.all_gather(values, "row", axis=0, tiled=True),
    )
    query_count = block_mask.shape[0]
    key_count = block_mask.shape[1]
    keep_most = max(2, 7 * key_count // 16)
    if query_count % 4 == 0:
        group_size = 4
    elif query_count % 2 == 0:
        group_size = 2
    else:
        group_size = 1
    key_blocks = key_tile.reshape(key_count, BLK, HEADS, HD)
    value_blocks = value_tile.reshape(key_count, BLK, HEADS, HD)
    within = jnp.arange(key_count, dtype=jnp.int32)
    priority = block_mask * (2 * key_count) + (key_count - within)[None, :]
    top_values, chosen = lax.top_k(priority, keep_most)
    usable = jnp.take_along_axis(block_mask, chosen, axis=1) > 0
    steps_count = query_count // group_size
    query_groups = query_tile.reshape(steps_count, group_size, BLK, HEADS, HD)
    chosen_groups = chosen.reshape(steps_count, group_size, keep_most)
    usable_groups = usable.reshape(steps_count, group_size, keep_most)

    def one_step(operands):
        query_rows, picked, allowed = operands
        near_keys = key_blocks[picked]
        near_values = value_blocks[picked]
        scores = (
            jnp.einsum(
                "gqhd,gkbhd->gqhkb", query_rows, near_keys, preferred_element_type=jnp.float32
            )
            * score_scale
        )
        scores = jnp.where(allowed[:, None, None, :, None], scores, -jnp.inf)
        tile_max = jnp.max(scores, axis=(3, 4))
        weights = jnp.exp(scores - tile_max[:, :, :, None, None])
        tile_total = jnp.sum(weights, axis=(3, 4))
        rounded = weights.astype(jnp.bfloat16)
        tile_sum = jnp.einsum(
            "gqhkb,gkbhd->gqhd", rounded, near_values, preferred_element_type=jnp.float32
        )
        return (tile_sum, tile_max, tile_total)

    tile_sum, tile_max, tile_total = lax.map(one_step, (query_groups, chosen_groups, usable_groups))
    query_rows_all = query_count * BLK
    tile_sum = tile_sum.reshape(query_rows_all, HEADS, HD)
    tile_max = tile_max.reshape(query_rows_all, HEADS)
    tile_total = tile_total.reshape(query_rows_all, HEADS)
    col_count = lax.axis_size("col")
    own_rows = query_rows_all // col_count
    moved_sum, moved_max, moved_total = (
        lax.all_to_all(
            tile_sum.reshape(col_count, own_rows, HEADS * HD),
            "col",
            split_axis=0,
            concat_axis=0,
            tiled=True,
        ),
        lax.all_to_all(
            tile_max.reshape(col_count, own_rows, HEADS),
            "col",
            split_axis=0,
            concat_axis=0,
            tiled=True,
        ),
        lax.all_to_all(
            tile_total.reshape(col_count, own_rows, HEADS),
            "col",
            split_axis=0,
            concat_axis=0,
            tiled=True,
        ),
    )
    row_max = jnp.max(moved_max, axis=0)
    factor = jnp.exp(moved_max - row_max[None, :, :])
    numer = jnp.sum(
        moved_sum.reshape(col_count, own_rows, HEADS, HD) * factor[:, :, :, None], axis=0
    )
    denom = jnp.sum(moved_total * factor, axis=0)
    attended = (numer / denom[:, :, None]).reshape(own_rows, HEADS * HD).astype(jnp.bfloat16)
    projected = jnp.dot(
        attended,
        lax.all_gather(out_weight, ("row", "col"), axis=1, tiled=True),
        preferred_element_type=jnp.float32,
    )
    return (projected + residual.astype(jnp.float32)).astype(jnp.bfloat16)


def fused_kernel(
    slots, q_in, k_in, v_in, mask_in, w_in, res_in, out_ref,
    qbuf, kv, wt, mask, psend, precv, ssend, srecv,
    osum, spread_scale, res, blank, load_sem, send_sem, recv_sem,
):
    score_scale = 1.0 / math.sqrt(HD)
    g = lax.axis_index("groups")
    r = lax.axis_index("row")
    c = lax.axis_index("col")
    rows, cols = wt.shape[0], wt.shape[1]
    r_chip = lax.rem(r + 2, rows)
    r_core = r + 1 - 2 * lax.rem(r, 2)
    r_both = r_chip + 1 - 2 * lax.rem(r, 2)
    other = 1 - g
    chip = {"row": r_chip}
    core = {"row": r_core}
    video = {"groups": other}
    diagonal = {"groups": other, "row": r_chip}

    loads = [
        pltpu.make_async_copy(q_in, qbuf.at[0], load_sem.at[0]),
        pltpu.make_async_copy(k_in, kv.at[r, 0], load_sem.at[1]),
        pltpu.make_async_copy(v_in, kv.at[r, 1], load_sem.at[2]),
        pltpu.make_async_copy(w_in, wt.at[r, c], load_sem.at[3]),
        pltpu.make_async_copy(mask_in, mask, load_sem.at[4]),
        pltpu.make_async_copy(res_in, res, load_sem.at[5]),
    ]
    for load in loads:
        load.start()

    barrier = pltpu.get_barrier_semaphore()
    peers = [{"col": lax.rem(c + j, cols)} for j in range(1, cols)] + [chip, core, video, diagonal]
    for peer in peers:
        pl.semaphore_signal(barrier, inc=1, device_id=peer, device_id_type=MESH)
    pl.semaphore_wait(barrier, len(peers))

    bytes_of = {}
    names = []

    def send(src, dst, device, name):
        if name not in bytes_of:
            names.append(name)
            bytes_of[name] = 0
        size = math.prod(dst.shape) * dst.dtype.itemsize
        bytes_of[name] += size
        bytes_of[""] = bytes_of.get("", 0) + size
        pltpu.make_async_remote_copy(
            src_ref=src, dst_ref=dst,
            send_sem=send_sem, recv_sem=recv_sem.at[names.index(name)],
            device_id=device, device_id_type=MESH,
        ).start()

    def settle(sem, size):
        view = blank.at[pl.ds(0, size // (2 * BLK)), :]
        pltpu.make_async_copy(view, view, sem).wait()

    def wait(name):
        settle(recv_sem.at[names.index(name)], bytes_of[name])

    pair = c + 1 - 2 * lax.rem(c, 2)
    across = lax.rem(c + 2, cols)
    far = lax.rem(pair + 2, cols)
    targets = [pair, across, far]

    own = qbuf.shape[1]
    key_count = mask.shape[1]
    attended = []
    home = lax.div(c * own, BLK)
    first = lax.broadcasted_iota(jnp.int32, (BLK, 2 * own), 1) < own

    def visible(slot, j):
        block = home if slot < 2 else 1 - home
        return jnp.where(block == 0, mask[0:1, j : j + 1], mask[1:2, j : j + 1])

    def attend(near, late):
        pair_rows = [qbuf[near], qbuf[late]]
        seen = jnp.concatenate(
            [jnp.where(first, visible(near, j), visible(late, j)) for j in range(key_count)], axis=0
        )
        for h in range(HEADS):
            lanes = slice(h * HD, (h + 1) * HD)
            key_rows = kv[:, 0, :, lanes].reshape(-1, HD)
            value_rows = kv[:, 1, :, lanes].reshape(-1, HD)
            query_rows = jnp.concatenate([rows[:, lanes] for rows in pair_rows], axis=0)
            scores = lax.dot_general(
                key_rows, query_rows, (((1,), (1,)), ((), ())), preferred_element_type=jnp.float32
            )
            scores = jnp.where(seen > 0, scores * score_scale, -jnp.inf)
            tile_max = jnp.max(scores, axis=0, keepdims=True)
            weights = jnp.exp(scores - tile_max)
            tile_total = jnp.sum(weights, axis=0, keepdims=True)
            tile_sum = lax.dot_general(
                weights.astype(jnp.bfloat16), value_rows, (((0,), (0,)), ((), ())),
                preferred_element_type=jnp.float32,
            )
            for i, slot in enumerate((near, late)):
                part = slice(i * own, (i + 1) * own)
                ssend[slot, h : h + 1, 0:own] = tile_max[:, part]
                ssend[slot, HEADS + h : HEADS + h + 1, 0:own] = tile_total[:, part]
                if slot == 0:
                    osum[:, lanes] = tile_sum[part]
                else:
                    psend[slot - 1, :, lanes] = tile_sum[part].astype(jnp.bfloat16)
        for slot in (near, late):
            if slot > 0:
                send(ssend.at[slot], srecv.at[slot - 1], {"col": targets[slot - 1]}, "s")
                send(psend.at[slot - 1], precv.at[slot - 1], {"col": targets[slot - 1]}, "p")

    def prepare():
        wait("s")
        stats = [ssend[0]] + [srecv[t] for t in range(cols - 1)]
        maxes = [s[0:HEADS, :] for s in stats]
        totals = [s[HEADS : 2 * HEADS, :] for s in stats]
        row_max = functools.reduce(jnp.maximum, maxes)
        factors = [jnp.exp(m - row_max) for m in maxes]
        denom = functools.reduce(jnp.add, [t * f for t, f in zip(totals, factors)])
        pad = [jnp.zeros((8 - HEADS, denom.shape[1]), jnp.float32)]
        table = jnp.concatenate([x for f in factors for x in [f / denom] + pad], axis=0)
        fill = jnp.zeros((table.shape[1] - table.shape[0], table.shape[1]), jnp.float32)
        table = jnp.concatenate([table, fill], axis=0).T[0:own]
        for t in range(cols):
            for h in range(HEADS):
                column = table[:, 8 * t + h : 8 * t + h + 1]
                spread_scale[t, h] = jnp.broadcast_to(column, (own, HD))
        for h in range(HEADS):
            lanes = slice(h * HD, (h + 1) * HD)
            osum[:, lanes] = osum[:, lanes] * spread_scale[0, h]
        loads[5].wait()

    def merge():
        wait("p")
        heads = []
        for h in range(HEADS):
            lanes = slice(h * HD, (h + 1) * HD)
            mixed = osum[:, lanes]
            for t in range(1, cols):
                mixed += precv[t - 1, :, lanes].astype(jnp.float32) * spread_scale[t, h]
            heads.append(mixed)
        attended.append(jnp.concatenate(heads, axis=1).astype(jnp.bfloat16))

    width = cols * 2 * wt.shape[3]

    def project(row):
        columns = pl.ds(pl.multiple_of(row * width, BLK), width)
        projected = lax.dot_general(
            attended[0], wt[row].reshape(width, HEADS * HD), (((1,), (1,)), ((), ())),
            preferred_element_type=jnp.float32,
        )
        total = projected + res[:, columns].astype(jnp.float32)
        out_ref[:, columns] = total.astype(jnp.bfloat16)

    loads[3].wait()
    send(wt.at[r, c, g], wt.at[r, c, g], {"col": across}, "across")
    send(wt.at[r, c, g], wt.at[r, c, g], {"col": pair}, "pair")
    loads[0].wait()
    send(qbuf.at[0], qbuf.at[3], {"col": far}, "q_far")
    send(qbuf.at[0], qbuf.at[2], {"col": across}, "q_across")
    send(qbuf.at[0], qbuf.at[1], {"col": pair}, "q_pair")
    loads[1].wait()
    loads[2].wait()
    send(kv.at[r], kv.at[r], chip, "kv_chip")
    send(kv.at[r], kv.at[r], core, "kv_core")
    send(wt.at[r, c], wt.at[r, c], core, "core_r")
    wait("kv_chip")
    send(kv.at[r_chip], kv.at[r_chip], core, "kv_core")
    send(wt.at[r, c], wt.at[r, c], chip, "own_x")
    wait("across")
    send(wt.at[r, across, g], wt.at[r, across, g], {"col": pair}, "far")
    send(wt.at[r, across, g], wt.at[r, across, g], video, "across_y")
    send(wt.at[r, across, g], wt.at[r, across, g], chip, "across_x")
    send(wt.at[r, across, g], wt.at[r, across, g], core, "core_r")
    wait("pair")
    send(wt.at[r, pair, g], wt.at[r, pair, g], video, "pair_y")
    send(wt.at[r, pair, g], wt.at[r, pair, g], diagonal, "pair_d")
    send(wt.at[r, pair, g], wt.at[r, pair, g], chip, "pair_x")
    send(wt.at[r, pair, g], wt.at[r, pair, g], core, "core_r")
    wait("q_far")
    wait("q_across")
    wait("kv_core")
    loads[4].wait()
    attend(2, 3)
    wait("q_pair")
    attend(1, 0)
    wait("far")
    send(wt.at[r, far, g], wt.at[r, far, g], video, "far_y")
    send(wt.at[r, far, g], wt.at[r, far, g], diagonal, "far_d")
    send(wt.at[r, far, g], wt.at[r, far, g], chip, "far_x")
    send(wt.at[r, far, g], wt.at[r, far, g], core, "core_r")
    wait("across_y")
    send(wt.at[r, across, other], wt.at[r, across, other], core, "core_r")
    send(wt.at[r, across, other], wt.at[r, across, other], chip, "across_d")
    wait("across_x")
    send(wt.at[r_chip, across, g], wt.at[r_chip, across, g], core, "core_x")
    wait("own_x")
    send(wt.at[r_chip, c], wt.at[r_chip, c], core, "core_x")
    wait("pair_y")
    send(wt.at[r, pair, other], wt.at[r, pair, other], core, "core_r")
    wait("pair_x")
    send(wt.at[r_chip, pair, g], wt.at[r_chip, pair, g], core, "core_x")
    wait("pair_d")
    send(wt.at[r_chip, pair, other], wt.at[r_chip, pair, other], core, "core_x")
    wait("far_y")
    send(wt.at[r, far, other], wt.at[r, far, other], core, "core_r")
    prepare()
    merge()
    project(r)
    wait("far_x")
    send(wt.at[r_chip, far, g], wt.at[r_chip, far, g], core, "core_x")
    wait("far_d")
    send(wt.at[r_chip, far, other], wt.at[r_chip, far, other], core, "core_x")
    wait("across_d")
    send(wt.at[r_chip, across, other], wt.at[r_chip, across, other], core, "core_x")
    project(r_chip)
    wait("core_r")
    project(r_core)
    wait("core_x")
    project(r_both)
    assert len(names) == slots, len(names)
    settle(send_sem, bytes_of[""])


def fused(queries, keys, values, block_mask, out_weight, residual):
    rows, cols = lax.axis_size("row"), lax.axis_size("col")
    own, width = queries.shape
    depth, part = out_weight.shape
    slots = 22
    any_space = pl.BlockSpec(memory_space=pl.ANY)
    return pl.pallas_call(
        functools.partial(fused_kernel, slots),
        out_shape=pltpu.VMEM((own, residual.shape[1]), jnp.bfloat16),
        in_specs=[any_space] * 6,
        out_specs=pl.BlockSpec(memory_space=pltpu.VMEM),
        scratch_shapes=[
            pltpu.VMEM((cols, own, width), jnp.bfloat16),
            pltpu.VMEM((rows, 2, own, width), jnp.bfloat16),
            pltpu.VMEM((rows, cols, 2, part // 2, depth), jnp.bfloat16),
            pltpu.VMEM(block_mask.shape, jnp.int32),
            pltpu.VMEM((cols - 1, own, width), jnp.bfloat16),
            pltpu.VMEM((cols - 1, own, width), jnp.bfloat16),
            pltpu.VMEM((cols, 8, BLK), jnp.float32),
            pltpu.VMEM((cols - 1, 8, BLK), jnp.float32),
            pltpu.VMEM((own, width), jnp.float32),
            pltpu.VMEM((cols, HEADS, own, HD), jnp.float32),
            pltpu.VMEM(residual.shape, jnp.bfloat16),
            pltpu.VMEM((rows * cols * 2 * part * depth // BLK, BLK), jnp.bfloat16),
            pltpu.SemaphoreType.DMA((6,)),
            pltpu.SemaphoreType.DMA,
            pltpu.SemaphoreType.DMA((slots,)),
        ],
        compiler_params=pltpu.CompilerParams(collective_id=0, has_side_effects=True),
    )(queries, keys, values, block_mask, out_weight.T.reshape(2, part // 2, depth), residual)


def kernel_fits(mesh):
    return mesh.shape["groups"] == 2 and mesh.shape["row"] == 4 and mesh.shape["col"] == 4


def solution(mesh):
    body = fused if kernel_fits(mesh) else local
    placed = (
        P(("groups", "row", "col"), None),
        P(("groups", "col", "row"), None),
        P(("groups", "col", "row"), None),
        P(("groups", "row"), "col"),
        P(None, ("row", "col")),
        P(("groups", "row", "col"), None),
    )
    return jax.shard_map(
        body,
        mesh=mesh,
        in_specs=placed,
        out_specs=P(("groups", "row", "col"), None),
        check_vma=False,
    )
```

```python
import functools
import math

import jax
import jax.numpy as jnp
from jax import lax
from jax.experimental import pallas as pl
from jax.experimental.pallas import tpu as pltpu
from jax.sharding import PartitionSpec as P

HD = 128
HEADS = 3
BLK = 128
MESH = pl.DeviceIdType.MESH


def local(queries, keys, values, block_mask, out_weight, residual):
    score_scale = 1.0 / math.sqrt(HD)
    query_tile = lax.all_gather(queries, "col", axis=0, tiled=True)
    key_tile, value_tile = (
        lax.all_gather(keys, "row", axis=0, tiled=True),
        lax.all_gather(values, "row", axis=0, tiled=True),
    )
    query_count = block_mask.shape[0]
    key_count = block_mask.shape[1]
    keep_most = max(2, 7 * key_count // 16)
    if query_count % 4 == 0:
        group_size = 4
    elif query_count % 2 == 0:
        group_size = 2
    else:
        group_size = 1
    key_blocks = key_tile.reshape(key_count, BLK, HEADS, HD)
    value_blocks = value_tile.reshape(key_count, BLK, HEADS, HD)
    within = jnp.arange(key_count, dtype=jnp.int32)
    priority = block_mask * (2 * key_count) + (key_count - within)[None, :]
    top_values, chosen = lax.top_k(priority, keep_most)
    usable = jnp.take_along_axis(block_mask, chosen, axis=1) > 0
    steps_count = query_count // group_size
    query_groups = query_tile.reshape(steps_count, group_size, BLK, HEADS, HD)
    chosen_groups = chosen.reshape(steps_count, group_size, keep_most)
    usable_groups = usable.reshape(steps_count, group_size, keep_most)

    def one_step(operands):
        query_rows, picked, allowed = operands
        near_keys = key_blocks[picked]
        near_values = value_blocks[picked]
        scores = (
            jnp.einsum(
                "gqhd,gkbhd->gqhkb", query_rows, near_keys, preferred_element_type=jnp.float32
            )
            * score_scale
        )
        scores = jnp.where(allowed[:, None, None, :, None], scores, -jnp.inf)
        tile_max = jnp.max(scores, axis=(3, 4))
        weights = jnp.exp(scores - tile_max[:, :, :, None, None])
        tile_total = jnp.sum(weights, axis=(3, 4))
        rounded = weights.astype(jnp.bfloat16)
        tile_sum = jnp.einsum(
            "gqhkb,gkbhd->gqhd", rounded, near_values, preferred_element_type=jnp.float32
        )
        return (tile_sum, tile_max, tile_total)

    tile_sum, tile_max, tile_total = lax.map(one_step, (query_groups, chosen_groups, usable_groups))
    query_rows_all = query_count * BLK
    tile_sum = tile_sum.reshape(query_rows_all, HEADS, HD)
    tile_max = tile_max.reshape(query_rows_all, HEADS)
    tile_total = tile_total.reshape(query_rows_all, HEADS)
    col_count = lax.axis_size("col")
    own_rows = query_rows_all // col_count
    moved_sum, moved_max, moved_total = (
        lax.all_to_all(
            tile_sum.reshape(col_count, own_rows, HEADS * HD),
            "col",
            split_axis=0,
            concat_axis=0,
            tiled=True,
        ),
        lax.all_to_all(
            tile_max.reshape(col_count, own_rows, HEADS),
            "col",
            split_axis=0,
            concat_axis=0,
            tiled=True,
        ),
        lax.all_to_all(
            tile_total.reshape(col_count, own_rows, HEADS),
            "col",
            split_axis=0,
            concat_axis=0,
            tiled=True,
        ),
    )
    row_max = jnp.max(moved_max, axis=0)
    factor = jnp.exp(moved_max - row_max[None, :, :])
    numer = jnp.sum(
        moved_sum.reshape(col_count, own_rows, HEADS, HD) * factor[:, :, :, None], axis=0
    )
    denom = jnp.sum(moved_total * factor, axis=0)
    attended = (numer / denom[:, :, None]).reshape(own_rows, HEADS * HD).astype(jnp.bfloat16)
    projected = jnp.dot(
        attended,
        lax.all_gather(out_weight, ("row", "col"), axis=1, tiled=True),
        preferred_element_type=jnp.float32,
    )
    return (projected + residual.astype(jnp.float32)).astype(jnp.bfloat16)


def fused_kernel(
    slots, q_in, k_in, v_in, mask_in, w_in, res_in, out_ref,
    qbuf, kv, wt, mask, psend, precv, ssend, srecv,
    osum, spread_scale, res, blank, load_sem, send_sem, recv_sem,
):
    score_scale = 1.0 / math.sqrt(HD)
    g = lax.axis_index("groups")
    r = lax.axis_index("row")
    c = lax.axis_index("col")
    rows, cols = wt.shape[0], wt.shape[1]
    r_chip = lax.rem(r + 2, rows)
    r_core = r + 1 - 2 * lax.rem(r, 2)
    r_both = r_chip + 1 - 2 * lax.rem(r, 2)
    other = 1 - g
    chip = {"row": r_chip}
    core = {"row": r_core}
    video = {"groups": other}
    diagonal = {"groups": other, "row": r_chip}

    loads = [
        pltpu.make_async_copy(q_in, qbuf.at[0], load_sem.at[0]),
        pltpu.make_async_copy(k_in, kv.at[r, 0], load_sem.at[1]),
        pltpu.make_async_copy(v_in, kv.at[r, 1], load_sem.at[2]),
        pltpu.make_async_copy(w_in, wt.at[r, c], load_sem.at[3]),
        pltpu.make_async_copy(mask_in, mask, load_sem.at[4]),
        pltpu.make_async_copy(res_in, res, load_sem.at[5]),
    ]
    for load in loads:
        load.start()

    barrier = pltpu.get_barrier_semaphore()
    peers = [{"col": lax.rem(c + j, cols)} for j in range(1, cols)] + [chip, core, video, diagonal]
    for peer in peers:
        pl.semaphore_signal(barrier, inc=1, device_id=peer, device_id_type=MESH)
    pl.semaphore_wait(barrier, len(peers))

    bytes_of = {}
    names = []

    def send(src, dst, device, name):
        if name not in bytes_of:
            names.append(name)
            bytes_of[name] = 0
        size = math.prod(dst.shape) * dst.dtype.itemsize
        bytes_of[name] += size
        bytes_of[""] = bytes_of.get("", 0) + size
        pltpu.make_async_remote_copy(
            src_ref=src, dst_ref=dst,
            send_sem=send_sem, recv_sem=recv_sem.at[names.index(name)],
            device_id=device, device_id_type=MESH,
        ).start()

    def settle(sem, size):
        view = blank.at[pl.ds(0, size // (2 * BLK)), :]
        pltpu.make_async_copy(view, view, sem).wait()

    def wait(name):
        settle(recv_sem.at[names.index(name)], bytes_of[name])

    pair = c + 1 - 2 * lax.rem(c, 2)
    across = lax.rem(c + 2, cols)
    far = lax.rem(pair + 2, cols)
    targets = [pair, across, far]

    own = qbuf.shape[1]
    key_count = mask.shape[1]
    attended = []
    home = lax.div(c * own, BLK)
    first = lax.broadcasted_iota(jnp.int32, (BLK, 2 * own), 1) < own

    def visible(slot, j):
        block = home if slot < 2 else 1 - home
        return jnp.where(block == 0, mask[0:1, j : j + 1], mask[1:2, j : j + 1])

    def attend(near, late):
        pair_rows = [qbuf[near], qbuf[late]]
        seen = jnp.concatenate(
            [jnp.where(first, visible(near, j), visible(late, j)) for j in range(key_count)], axis=0
        )
        for h in range(HEADS):
            lanes = slice(h * HD, (h + 1) * HD)
            key_rows = kv[:, 0, :, lanes].reshape(-1, HD)
            value_rows = kv[:, 1, :, lanes].reshape(-1, HD)
            query_rows = jnp.concatenate([rows[:, lanes] for rows in pair_rows], axis=0)
            scores = lax.dot_general(
                key_rows, query_rows, (((1,), (1,)), ((), ())), preferred_element_type=jnp.float32
            )
            scores = jnp.where(seen > 0, scores * score_scale, -jnp.inf)
            tile_max = jnp.max(scores, axis=0, keepdims=True)
            weights = jnp.exp(scores - tile_max)
            tile_total = jnp.sum(weights, axis=0, keepdims=True)
            tile_sum = lax.dot_general(
                weights.astype(jnp.bfloat16), value_rows, (((0,), (0,)), ((), ())),
                preferred_element_type=jnp.float32,
            )
            for i, slot in enumerate((near, late)):
                part = slice(i * own, (i + 1) * own)
                ssend[slot, h : h + 1, 0:own] = tile_max[:, part]
                ssend[slot, HEADS + h : HEADS + h + 1, 0:own] = tile_total[:, part]
                if slot == 0:
                    osum[:, lanes] = tile_sum[part]
                else:
                    psend[slot - 1, :, lanes] = tile_sum[part].astype(jnp.bfloat16)
        for slot in (near, late):
            if slot > 0:
                send(ssend.at[slot], srecv.at[slot - 1], {"col": targets[slot - 1]}, "s")
                send(psend.at[slot - 1], precv.at[slot - 1], {"col": targets[slot - 1]}, "p")

    def prepare():
        wait("s")
        stats = [ssend[0]] + [srecv[t] for t in range(cols - 1)]
        maxes = [s[0:HEADS, :] for s in stats]
        totals = [s[HEADS : 2 * HEADS, :] for s in stats]
        row_max = functools.reduce(jnp.maximum, maxes)
        factors = [jnp.exp(m - row_max) for m in maxes]
        denom = functools.reduce(jnp.add, [t * f for t, f in zip(totals, factors)])
        pad = [jnp.zeros((8 - HEADS, denom.shape[1]), jnp.float32)]
        table = jnp.concatenate([x for f in factors for x in [f / denom] + pad], axis=0)
        fill = jnp.zeros((table.shape[1] - table.shape[0], table.shape[1]), jnp.float32)
        table = jnp.concatenate([table, fill], axis=0).T[0:own]
        for t in range(cols):
            for h in range(HEADS):
                column = table[:, 8 * t + h : 8 * t + h + 1]
                spread_scale[t, h] = jnp.broadcast_to(column, (own, HD))
        for h in range(HEADS):
            lanes = slice(h * HD, (h + 1) * HD)
            osum[:, lanes] = osum[:, lanes] * spread_scale[0, h]
        loads[5].wait()

    def merge():
        wait("p")
        heads = []
        for h in range(HEADS):
            lanes = slice(h * HD, (h + 1) * HD)
            mixed = osum[:, lanes]
            for t in range(1, cols):
                mixed += precv[t - 1, :, lanes].astype(jnp.float32) * spread_scale[t, h]
            heads.append(mixed)
        attended.append(jnp.concatenate(heads, axis=1).astype(jnp.bfloat16))

    width = cols * 2 * wt.shape[3]

    def project(row):
        columns = pl.ds(pl.multiple_of(row * width, BLK), width)
        projected = lax.dot_general(
            attended[0], wt[row].reshape(width, HEADS * HD), (((1,), (1,)), ((), ())),
            preferred_element_type=jnp.float32,
        )
        total = projected + res[:, columns].astype(jnp.float32)
        out_ref[:, columns] = total.astype(jnp.bfloat16)

    loads[3].wait()
    send(wt.at[r, c, g], wt.at[r, c, g], {"col": across}, "across")
    send(wt.at[r, c, g], wt.at[r, c, g], {"col": pair}, "pair")
    loads[0].wait()
    send(qbuf.at[0], qbuf.at[3], {"col": far}, "q_far")
    send(qbuf.at[0], qbuf.at[2], {"col": across}, "q_across")
    send(qbuf.at[0], qbuf.at[1], {"col": pair}, "q_pair")
    loads[1].wait()
    loads[2].wait()
    send(kv.at[r], kv.at[r], chip, "kv_chip")
    send(kv.at[r], kv.at[r], core, "kv_core")
    send(wt.at[r, c], wt.at[r, c], core, "core_r")
    wait("kv_chip")
    send(kv.at[r_chip], kv.at[r_chip], core, "kv_core")
    send(wt.at[r, c], wt.at[r, c], chip, "own_x")
    wait("pair")
    send(wt.at[r, pair, g], wt.at[r, pair, g], video, "pair_y")
    send(wt.at[r, pair, g], wt.at[r, pair, g], chip, "pair_x")
    send(wt.at[r, pair, g], wt.at[r, pair, g], core, "core_r")
    wait("across")
    send(wt.at[r, across, g], wt.at[r, across, g], {"col": pair}, "far")
    send(wt.at[r, across, g], wt.at[r, across, g], chip, "across_x")
    send(wt.at[r, across, g], wt.at[r, across, g], video, "across_y")
    send(wt.at[r, across, g], wt.at[r, across, g], core, "core_r")
    wait("q_far")
    wait("q_across")
    wait("kv_core")
    loads[4].wait()
    attend(2, 3)
    wait("pair_y")
    send(wt.at[r, pair, other], wt.at[r, pair, other], core, "core_r")
    send(wt.at[r, pair, other], wt.at[r, pair, other], chip, "pair_d")
    wait("q_pair")
    attend(1, 0)
    wait("far")
    send(wt.at[r, far, g], wt.at[r, far, g], video, "far_y")
    send(wt.at[r, far, g], wt.at[r, far, g], diagonal, "far_d")
    send(wt.at[r, far, g], wt.at[r, far, g], chip, "far_x")
    send(wt.at[r, far, g], wt.at[r, far, g], core, "core_r")
    wait("across_x")
    send(wt.at[r_chip, across, g], wt.at[r_chip, across, g], core, "core_x")
    send(wt.at[r_chip, across, g], wt.at[r_chip, across, g], video, "across_d")
    wait("own_x")
    send(wt.at[r_chip, c], wt.at[r_chip, c], core, "core_x")
    wait("across_y")
    send(wt.at[r, across, other], wt.at[r, across, other], core, "core_r")
    wait("pair_x")
    send(wt.at[r_chip, pair, g], wt.at[r_chip, pair, g], core, "core_x")
    wait("pair_d")
    send(wt.at[r_chip, pair, other], wt.at[r_chip, pair, other], core, "core_x")
    wait("far_y")
    send(wt.at[r, far, other], wt.at[r, far, other], core, "core_r")
    prepare()
    merge()
    project(r)
    wait("far_x")
    send(wt.at[r_chip, far, g], wt.at[r_chip, far, g], core, "core_x")
    wait("far_d")
    send(wt.at[r_chip, far, other], wt.at[r_chip, far, other], core, "core_x")
    wait("across_d")
    send(wt.at[r_chip, across, other], wt.at[r_chip, across, other], core, "core_x")
    project(r_chip)
    wait("core_r")
    project(r_core)
    wait("core_x")
    project(r_both)
    assert len(names) == slots, len(names)
    settle(send_sem, bytes_of[""])


def fused(queries, keys, values, block_mask, out_weight, residual):
    rows, cols = lax.axis_size("row"), lax.axis_size("col")
    own, width = queries.shape
    depth, part = out_weight.shape
    slots = 22
    any_space = pl.BlockSpec(memory_space=pl.ANY)
    return pl.pallas_call(
        functools.partial(fused_kernel, slots),
        out_shape=pltpu.VMEM((own, residual.shape[1]), jnp.bfloat16),
        in_specs=[any_space] * 6,
        out_specs=pl.BlockSpec(memory_space=pltpu.VMEM),
        scratch_shapes=[
            pltpu.VMEM((cols, own, width), jnp.bfloat16),
            pltpu.VMEM((rows, 2, own, width), jnp.bfloat16),
            pltpu.VMEM((rows, cols, 2, part // 2, depth), jnp.bfloat16),
            pltpu.VMEM(block_mask.shape, jnp.int32),
            pltpu.VMEM((cols - 1, own, width), jnp.bfloat16),
            pltpu.VMEM((cols - 1, own, width), jnp.bfloat16),
            pltpu.VMEM((cols, 8, BLK), jnp.float32),
            pltpu.VMEM((cols - 1, 8, BLK), jnp.float32),
            pltpu.VMEM((own, width), jnp.float32),
            pltpu.VMEM((cols, HEADS, own, HD), jnp.float32),
            pltpu.VMEM(residual.shape, jnp.bfloat16),
            pltpu.VMEM((rows * cols * 2 * part * depth // BLK, BLK), jnp.bfloat16),
            pltpu.SemaphoreType.DMA((6,)),
            pltpu.SemaphoreType.DMA,
            pltpu.SemaphoreType.DMA((slots,)),
        ],
        compiler_params=pltpu.CompilerParams(collective_id=0, has_side_effects=True),
    )(queries, keys, values, block_mask, out_weight.T.reshape(2, part // 2, depth), residual)


def kernel_fits(mesh):
    return mesh.shape["groups"] == 2 and mesh.shape["row"] == 4 and mesh.shape["col"] == 4


def solution(mesh):
    body = fused if kernel_fits(mesh) else local
    placed = (
        P(("groups", "row", "col"), None),
        P(("groups", "col", "row"), None),
        P(("groups", "col", "row"), None),
        P(("groups", "row"), "col"),
        P(None, ("row", "col")),
        P(("groups", "row", "col"), None),
    )
    return jax.shard_map(
        body,
        mesh=mesh,
        in_specs=placed,
        out_specs=P(("groups", "row", "col"), None),
        check_vma=False,
    )
```

```python
import functools
import math

import jax
import jax.numpy as jnp
from jax import lax
from jax.experimental import pallas as pl
from jax.experimental.pallas import tpu as pltpu
from jax.sharding import PartitionSpec as P

HD = 128
HEADS = 3
BLK = 128
MESH = pl.DeviceIdType.MESH


def local(queries, keys, values, block_mask, out_weight, residual):
    score_scale = 1.0 / math.sqrt(HD)
    query_tile = lax.all_gather(queries, "col", axis=0, tiled=True)
    key_tile, value_tile = (
        lax.all_gather(keys, "row", axis=0, tiled=True),
        lax.all_gather(values, "row", axis=0, tiled=True),
    )
    query_count = block_mask.shape[0]
    key_count = block_mask.shape[1]
    keep_most = max(2, 7 * key_count // 16)
    if query_count % 4 == 0:
        group_size = 4
    elif query_count % 2 == 0:
        group_size = 2
    else:
        group_size = 1
    key_blocks = key_tile.reshape(key_count, BLK, HEADS, HD)
    value_blocks = value_tile.reshape(key_count, BLK, HEADS, HD)
    within = jnp.arange(key_count, dtype=jnp.int32)
    priority = block_mask * (2 * key_count) + (key_count - within)[None, :]
    top_values, chosen = lax.top_k(priority, keep_most)
    usable = jnp.take_along_axis(block_mask, chosen, axis=1) > 0
    steps_count = query_count // group_size
    query_groups = query_tile.reshape(steps_count, group_size, BLK, HEADS, HD)
    chosen_groups = chosen.reshape(steps_count, group_size, keep_most)
    usable_groups = usable.reshape(steps_count, group_size, keep_most)

    def one_step(operands):
        query_rows, picked, allowed = operands
        near_keys = key_blocks[picked]
        near_values = value_blocks[picked]
        scores = (
            jnp.einsum(
                "gqhd,gkbhd->gqhkb", query_rows, near_keys, preferred_element_type=jnp.float32
            )
            * score_scale
        )
        scores = jnp.where(allowed[:, None, None, :, None], scores, -jnp.inf)
        tile_max = jnp.max(scores, axis=(3, 4))
        weights = jnp.exp(scores - tile_max[:, :, :, None, None])
        tile_total = jnp.sum(weights, axis=(3, 4))
        rounded = weights.astype(jnp.bfloat16)
        tile_sum = jnp.einsum(
            "gqhkb,gkbhd->gqhd", rounded, near_values, preferred_element_type=jnp.float32
        )
        return (tile_sum, tile_max, tile_total)

    tile_sum, tile_max, tile_total = lax.map(one_step, (query_groups, chosen_groups, usable_groups))
    query_rows_all = query_count * BLK
    tile_sum = tile_sum.reshape(query_rows_all, HEADS, HD)
    tile_max = tile_max.reshape(query_rows_all, HEADS)
    tile_total = tile_total.reshape(query_rows_all, HEADS)
    col_count = lax.axis_size("col")
    own_rows = query_rows_all // col_count
    moved_sum, moved_max, moved_total = (
        lax.all_to_all(
            tile_sum.reshape(col_count, own_rows, HEADS * HD),
            "col",
            split_axis=0,
            concat_axis=0,
            tiled=True,
        ),
        lax.all_to_all(
            tile_max.reshape(col_count, own_rows, HEADS),
            "col",
            split_axis=0,
            concat_axis=0,
            tiled=True,
        ),
        lax.all_to_all(
            tile_total.reshape(col_count, own_rows, HEADS),
            "col",
            split_axis=0,
            concat_axis=0,
            tiled=True,
        ),
    )
    row_max = jnp.max(moved_max, axis=0)
    factor = jnp.exp(moved_max - row_max[None, :, :])
    numer = jnp.sum(
        moved_sum.reshape(col_count, own_rows, HEADS, HD) * factor[:, :, :, None], axis=0
    )
    denom = jnp.sum(moved_total * factor, axis=0)
    attended = (numer / denom[:, :, None]).reshape(own_rows, HEADS * HD).astype(jnp.bfloat16)
    projected = jnp.dot(
        attended,
        lax.all_gather(out_weight, ("row", "col"), axis=1, tiled=True),
        preferred_element_type=jnp.float32,
    )
    return (projected + residual.astype(jnp.float32)).astype(jnp.bfloat16)


def fused_kernel(
    slots, q_in, k_in, v_in, mask_in, w_in, res_in, out_ref,
    qbuf, kv, wt, mask, psend, precv, ssend, srecv,
    osum, spread_scale, res, blank, load_sem, send_sem, recv_sem,
):
    score_scale = 1.0 / math.sqrt(HD)
    g = lax.axis_index("groups")
    r = lax.axis_index("row")
    c = lax.axis_index("col")
    rows, cols = wt.shape[0], wt.shape[1]
    r_chip = lax.rem(r + 2, rows)
    r_core = r + 1 - 2 * lax.rem(r, 2)
    r_both = r_chip + 1 - 2 * lax.rem(r, 2)
    other = 1 - g
    chip = {"row": r_chip}
    core = {"row": r_core}
    video = {"groups": other}
    diagonal = {"groups": other, "row": r_chip}

    loads = [
        pltpu.make_async_copy(q_in, qbuf.at[0], load_sem.at[0]),
        pltpu.make_async_copy(k_in, kv.at[r, 0], load_sem.at[1]),
        pltpu.make_async_copy(v_in, kv.at[r, 1], load_sem.at[2]),
        pltpu.make_async_copy(w_in, wt.at[r, c], load_sem.at[3]),
        pltpu.make_async_copy(mask_in, mask, load_sem.at[4]),
        pltpu.make_async_copy(res_in, res, load_sem.at[5]),
    ]
    for load in loads:
        load.start()

    barrier = pltpu.get_barrier_semaphore()
    peers = [{"col": lax.rem(c + j, cols)} for j in range(1, cols)] + [chip, core, video]
    for peer in peers:
        pl.semaphore_signal(barrier, inc=1, device_id=peer, device_id_type=MESH)
    pl.semaphore_wait(barrier, len(peers))

    bytes_of = {}
    names = []

    def send(src, dst, device, name):
        if name not in bytes_of:
            names.append(name)
            bytes_of[name] = 0
        size = math.prod(dst.shape) * dst.dtype.itemsize
        bytes_of[name] += size
        bytes_of[""] = bytes_of.get("", 0) + size
        pltpu.make_async_remote_copy(
            src_ref=src, dst_ref=dst,
            send_sem=send_sem, recv_sem=recv_sem.at[names.index(name)],
            device_id=device, device_id_type=MESH,
        ).start()

    def settle(sem, size):
        view = blank.at[pl.ds(0, size // (2 * BLK)), :]
        pltpu.make_async_copy(view, view, sem).wait()

    def wait(name):
        settle(recv_sem.at[names.index(name)], bytes_of[name])

    pair = c + 1 - 2 * lax.rem(c, 2)
    across = lax.rem(c + 2, cols)
    far = lax.rem(pair + 2, cols)
    targets = [pair, across, far]

    own = qbuf.shape[1]
    key_count = mask.shape[1]
    attended = []
    home = lax.div(c * own, BLK)
    first = lax.broadcasted_iota(jnp.int32, (BLK, 2 * own), 1) < own

    def visible(slot, j):
        block = home if slot < 2 else 1 - home
        return jnp.where(block == 0, mask[0:1, j : j + 1], mask[1:2, j : j + 1])

    def attend(near, late):
        pair_rows = [qbuf[near], qbuf[late]]
        seen = jnp.concatenate(
            [jnp.where(first, visible(near, j), visible(late, j)) for j in range(key_count)], axis=0
        )
        for h in range(HEADS):
            lanes = slice(h * HD, (h + 1) * HD)
            key_rows = kv[:, 0, :, lanes].reshape(-1, HD)
            value_rows = kv[:, 1, :, lanes].reshape(-1, HD)
            query_rows = jnp.concatenate([rows[:, lanes] for rows in pair_rows], axis=0)
            scores = lax.dot_general(
                key_rows, query_rows, (((1,), (1,)), ((), ())), preferred_element_type=jnp.float32
            )
            scores = jnp.where(seen > 0, scores * score_scale, -jnp.inf)
            tile_max = jnp.max(scores, axis=0, keepdims=True)
            weights = jnp.exp(scores - tile_max)
            tile_total = jnp.sum(weights, axis=0, keepdims=True)
            tile_sum = lax.dot_general(
                weights.astype(jnp.bfloat16), value_rows, (((0,), (0,)), ((), ())),
                preferred_element_type=jnp.float32,
            )
            for i, slot in enumerate((near, late)):
                part = slice(i * own, (i + 1) * own)
                ssend[slot, h : h + 1, 0:own] = tile_max[:, part]
                ssend[slot, HEADS + h : HEADS + h + 1, 0:own] = tile_total[:, part]
                if slot == 0:
                    osum[:, lanes] = tile_sum[part]
                else:
                    psend[slot - 1, :, lanes] = tile_sum[part].astype(jnp.bfloat16)
        for slot in (near, late):
            if slot > 0:
                send(ssend.at[slot], srecv.at[slot - 1], {"col": targets[slot - 1]}, "s")
                send(psend.at[slot - 1], precv.at[slot - 1], {"col": targets[slot - 1]}, "p")

    def prepare():
        wait("s")
        stats = [ssend[0]] + [srecv[t] for t in range(cols - 1)]
        maxes = [s[0:HEADS, :] for s in stats]
        totals = [s[HEADS : 2 * HEADS, :] for s in stats]
        row_max = functools.reduce(jnp.maximum, maxes)
        factors = [jnp.exp(m - row_max) for m in maxes]
        denom = functools.reduce(jnp.add, [t * f for t, f in zip(totals, factors)])
        pad = [jnp.zeros((8 - HEADS, denom.shape[1]), jnp.float32)]
        table = jnp.concatenate([x for f in factors for x in [f / denom] + pad], axis=0)
        fill = jnp.zeros((table.shape[1] - table.shape[0], table.shape[1]), jnp.float32)
        table = jnp.concatenate([table, fill], axis=0).T[0:own]
        for t in range(cols):
            for h in range(HEADS):
                column = table[:, 8 * t + h : 8 * t + h + 1]
                spread_scale[t, h] = jnp.broadcast_to(column, (own, HD))
        for h in range(HEADS):
            lanes = slice(h * HD, (h + 1) * HD)
            osum[:, lanes] = osum[:, lanes] * spread_scale[0, h]
        loads[5].wait()

    def merge():
        wait("p")
        heads = []
        for h in range(HEADS):
            lanes = slice(h * HD, (h + 1) * HD)
            mixed = osum[:, lanes]
            for t in range(1, cols):
                mixed += precv[t - 1, :, lanes].astype(jnp.float32) * spread_scale[t, h]
            heads.append(mixed)
        attended.append(jnp.concatenate(heads, axis=1).astype(jnp.bfloat16))

    width = cols * 2 * wt.shape[3]

    def project(row):
        columns = pl.ds(pl.multiple_of(row * width, BLK), width)
        projected = lax.dot_general(
            attended[0], wt[row].reshape(width, HEADS * HD), (((1,), (1,)), ((), ())),
            preferred_element_type=jnp.float32,
        )
        total = projected + res[:, columns].astype(jnp.float32)
        out_ref[:, columns] = total.astype(jnp.bfloat16)

    loads[3].wait()
    send(wt.at[r, c, g], wt.at[r, c, g], {"col": across}, "across")
    send(wt.at[r, c, g], wt.at[r, c, g], {"col": pair}, "pair")
    loads[0].wait()
    send(qbuf.at[0], qbuf.at[3], {"col": far}, "q_far")
    send(qbuf.at[0], qbuf.at[2], {"col": across}, "q_across")
    send(qbuf.at[0], qbuf.at[1], {"col": pair}, "q_pair")
    loads[1].wait()
    loads[2].wait()
    send(kv.at[r], kv.at[r], chip, "kv_chip")
    send(kv.at[r], kv.at[r], core, "kv_core")
    send(wt.at[r, c], wt.at[r, c], core, "core_r")
    send(wt.at[r, c, g], wt.at[r, c, g], chip, "own_x")
    wait("kv_chip")
    send(kv.at[r_chip], kv.at[r_chip], core, "kv_core")
    wait("pair")
    send(wt.at[r, pair, g], wt.at[r, pair, g], video, "pair_y")
    send(wt.at[r, pair, g], wt.at[r, pair, g], chip, "pair_x")
    send(wt.at[r, pair, g], wt.at[r, pair, g], core, "core_r")
    wait("across")
    send(wt.at[r, across, g], wt.at[r, across, g], {"col": pair}, "far")
    send(wt.at[r, across, g], wt.at[r, across, g], chip, "across_x")
    send(wt.at[r, across, g], wt.at[r, across, g], video, "across_y")
    send(wt.at[r, across, g], wt.at[r, across, g], core, "core_r")
    wait("own_x")
    send(wt.at[r_chip, c, g], wt.at[r_chip, c, g], core, "core_x")
    send(wt.at[r_chip, c, g], wt.at[r_chip, c, g], video, "own_y")
    wait("q_far")
    wait("q_across")
    wait("kv_core")
    loads[4].wait()
    attend(2, 3)
    wait("pair_y")
    send(wt.at[r, pair, other], wt.at[r, pair, other], core, "core_r")
    send(wt.at[r, pair, other], wt.at[r, pair, other], chip, "pair_d")
    wait("q_pair")
    attend(1, 0)
    wait("far")
    send(wt.at[r, far, g], wt.at[r, far, g], video, "far_y")
    send(wt.at[r, far, g], wt.at[r, far, g], diagonal, "far_d")
    send(wt.at[r, far, g], wt.at[r, far, g], chip, "far_x")
    send(wt.at[r, far, g], wt.at[r, far, g], core, "core_r")
    wait("across_x")
    send(wt.at[r_chip, across, g], wt.at[r_chip, across, g], core, "core_x")
    send(wt.at[r_chip, across, g], wt.at[r_chip, across, g], video, "across_d")
    wait("across_y")
    send(wt.at[r, across, other], wt.at[r, across, other], core, "core_r")
    wait("own_y")
    send(wt.at[r_chip, c, other], wt.at[r_chip, c, other], core, "core_x")
    wait("pair_x")
    send(wt.at[r_chip, pair, g], wt.at[r_chip, pair, g], core, "core_x")
    wait("pair_d")
    send(wt.at[r_chip, pair, other], wt.at[r_chip, pair, other], core, "core_x")
    wait("far_y")
    send(wt.at[r, far, other], wt.at[r, far, other], core, "core_r")
    prepare()
    merge()
    project(r)
    wait("far_x")
    send(wt.at[r_chip, far, g], wt.at[r_chip, far, g], core, "core_x")
    wait("far_d")
    send(wt.at[r_chip, far, other], wt.at[r_chip, far, other], core, "core_x")
    wait("across_d")
    send(wt.at[r_chip, across, other], wt.at[r_chip, across, other], core, "core_x")
    project(r_chip)
    wait("core_r")
    project(r_core)
    wait("core_x")
    project(r_both)
    assert len(names) == slots, len(names)
    settle(send_sem, bytes_of[""])


def fused(queries, keys, values, block_mask, out_weight, residual):
    rows, cols = lax.axis_size("row"), lax.axis_size("col")
    own, width = queries.shape
    depth, part = out_weight.shape
    slots = 23
    any_space = pl.BlockSpec(memory_space=pl.ANY)
    return pl.pallas_call(
        functools.partial(fused_kernel, slots),
        out_shape=pltpu.VMEM((own, residual.shape[1]), jnp.bfloat16),
        in_specs=[any_space] * 6,
        out_specs=pl.BlockSpec(memory_space=pltpu.VMEM),
        scratch_shapes=[
            pltpu.VMEM((cols, own, width), jnp.bfloat16),
            pltpu.VMEM((rows, 2, own, width), jnp.bfloat16),
            pltpu.VMEM((rows, cols, 2, part // 2, depth), jnp.bfloat16),
            pltpu.VMEM(block_mask.shape, jnp.int32),
            pltpu.VMEM((cols - 1, own, width), jnp.bfloat16),
            pltpu.VMEM((cols - 1, own, width), jnp.bfloat16),
            pltpu.VMEM((cols, 8, BLK), jnp.float32),
            pltpu.VMEM((cols - 1, 8, BLK), jnp.float32),
            pltpu.VMEM((own, width), jnp.float32),
            pltpu.VMEM((cols, HEADS, own, HD), jnp.float32),
            pltpu.VMEM(residual.shape, jnp.bfloat16),
            pltpu.VMEM((rows * cols * 2 * part * depth // BLK, BLK), jnp.bfloat16),
            pltpu.SemaphoreType.DMA((6,)),
            pltpu.SemaphoreType.DMA,
            pltpu.SemaphoreType.DMA((slots,)),
        ],
        compiler_params=pltpu.CompilerParams(collective_id=0, has_side_effects=True),
    )(queries, keys, values, block_mask, out_weight.T.reshape(2, part // 2, depth), residual)


def kernel_fits(mesh):
    return mesh.shape["groups"] == 2 and mesh.shape["row"] == 4 and mesh.shape["col"] == 4


def solution(mesh):
    body = fused if kernel_fits(mesh) else local
    placed = (
        P(("groups", "row", "col"), None),
        P(("groups", "col", "row"), None),
        P(("groups", "col", "row"), None),
        P(("groups", "row"), "col"),
        P(None, ("row", "col")),
        P(("groups", "row", "col"), None),
    )
    return jax.shard_map(
        body,
        mesh=mesh,
        in_specs=placed,
        out_specs=P(("groups", "row", "col"), None),
        check_vma=False,
    )
```

```python
import functools
import math

import jax
import jax.numpy as jnp
from jax import lax
from jax.experimental import pallas as pl
from jax.experimental.pallas import tpu as pltpu
from jax.sharding import PartitionSpec as P

HD = 128
HEADS = 3
BLK = 128
MESH = pl.DeviceIdType.MESH


def local(queries, keys, values, block_mask, out_weight, residual):
    score_scale = 1.0 / math.sqrt(HD)
    query_tile = lax.all_gather(queries, "col", axis=0, tiled=True)
    key_tile, value_tile = (
        lax.all_gather(keys, "row", axis=0, tiled=True),
        lax.all_gather(values, "row", axis=0, tiled=True),
    )
    query_count = block_mask.shape[0]
    key_count = block_mask.shape[1]
    keep_most = max(2, 7 * key_count // 16)
    if query_count % 4 == 0:
        group_size = 4
    elif query_count % 2 == 0:
        group_size = 2
    else:
        group_size = 1
    key_blocks = key_tile.reshape(key_count, BLK, HEADS, HD)
    value_blocks = value_tile.reshape(key_count, BLK, HEADS, HD)
    within = jnp.arange(key_count, dtype=jnp.int32)
    priority = block_mask * (2 * key_count) + (key_count - within)[None, :]
    top_values, chosen = lax.top_k(priority, keep_most)
    usable = jnp.take_along_axis(block_mask, chosen, axis=1) > 0
    steps_count = query_count // group_size
    query_groups = query_tile.reshape(steps_count, group_size, BLK, HEADS, HD)
    chosen_groups = chosen.reshape(steps_count, group_size, keep_most)
    usable_groups = usable.reshape(steps_count, group_size, keep_most)

    def one_step(operands):
        query_rows, picked, allowed = operands
        near_keys = key_blocks[picked]
        near_values = value_blocks[picked]
        scores = (
            jnp.einsum(
                "gqhd,gkbhd->gqhkb", query_rows, near_keys, preferred_element_type=jnp.float32
            )
            * score_scale
        )
        scores = jnp.where(allowed[:, None, None, :, None], scores, -jnp.inf)
        tile_max = jnp.max(scores, axis=(3, 4))
        weights = jnp.exp(scores - tile_max[:, :, :, None, None])
        tile_total = jnp.sum(weights, axis=(3, 4))
        rounded = weights.astype(jnp.bfloat16)
        tile_sum = jnp.einsum(
            "gqhkb,gkbhd->gqhd", rounded, near_values, preferred_element_type=jnp.float32
        )
        return (tile_sum, tile_max, tile_total)

    tile_sum, tile_max, tile_total = lax.map(one_step, (query_groups, chosen_groups, usable_groups))
    query_rows_all = query_count * BLK
    tile_sum = tile_sum.reshape(query_rows_all, HEADS, HD)
    tile_max = tile_max.reshape(query_rows_all, HEADS)
    tile_total = tile_total.reshape(query_rows_all, HEADS)
    col_count = lax.axis_size("col")
    own_rows = query_rows_all // col_count
    moved_sum, moved_max, moved_total = (
        lax.all_to_all(
            tile_sum.reshape(col_count, own_rows, HEADS * HD),
            "col",
            split_axis=0,
            concat_axis=0,
            tiled=True,
        ),
        lax.all_to_all(
            tile_max.reshape(col_count, own_rows, HEADS),
            "col",
            split_axis=0,
            concat_axis=0,
            tiled=True,
        ),
        lax.all_to_all(
            tile_total.reshape(col_count, own_rows, HEADS),
            "col",
            split_axis=0,
            concat_axis=0,
            tiled=True,
        ),
    )
    row_max = jnp.max(moved_max, axis=0)
    factor = jnp.exp(moved_max - row_max[None, :, :])
    numer = jnp.sum(
        moved_sum.reshape(col_count, own_rows, HEADS, HD) * factor[:, :, :, None], axis=0
    )
    denom = jnp.sum(moved_total * factor, axis=0)
    attended = (numer / denom[:, :, None]).reshape(own_rows, HEADS * HD).astype(jnp.bfloat16)
    projected = jnp.dot(
        attended,
        lax.all_gather(out_weight, ("row", "col"), axis=1, tiled=True),
        preferred_element_type=jnp.float32,
    )
    return (projected + residual.astype(jnp.float32)).astype(jnp.bfloat16)


def fused_kernel(
    slots, q_in, k_in, v_in, mask_in, w_in, res_in, out_ref,
    qbuf, kv, wt, mask, psend, precv, ssend, srecv,
    osum, spread_scale, res, blank, load_sem, send_sem, recv_sem,
):
    score_scale = 1.0 / math.sqrt(HD)
    g = lax.axis_index("groups")
    r = lax.axis_index("row")
    c = lax.axis_index("col")
    rows, cols = wt.shape[0], wt.shape[1]
    r_chip = lax.rem(r + 2, rows)
    r_core = r + 1 - 2 * lax.rem(r, 2)
    r_both = r_chip + 1 - 2 * lax.rem(r, 2)
    other = 1 - g
    chip = {"row": r_chip}
    core = {"row": r_core}
    video = {"groups": other}
    diagonal = {"groups": other, "row": r_chip}

    loads = [
        pltpu.make_async_copy(q_in, qbuf.at[0], load_sem.at[0]),
        pltpu.make_async_copy(k_in, kv.at[r, 0], load_sem.at[1]),
        pltpu.make_async_copy(v_in, kv.at[r, 1], load_sem.at[2]),
        pltpu.make_async_copy(w_in, wt.at[r, c], load_sem.at[3]),
        pltpu.make_async_copy(mask_in, mask, load_sem.at[4]),
        pltpu.make_async_copy(res_in, res, load_sem.at[5]),
    ]
    barrier = pltpu.get_barrier_semaphore()
    peers = [{"col": lax.rem(c + j, cols)} for j in range(1, cols)] + [chip, core, video]
    for peer in peers:
        pl.semaphore_signal(barrier, inc=1, device_id=peer, device_id_type=MESH)

    for load in loads:
        load.start()

    pl.semaphore_wait(barrier, len(peers))

    bytes_of = {}
    names = []

    def send(src, dst, device, name):
        if name not in bytes_of:
            names.append(name)
            bytes_of[name] = 0
        size = math.prod(dst.shape) * dst.dtype.itemsize
        bytes_of[name] += size
        bytes_of[""] = bytes_of.get("", 0) + size
        pltpu.make_async_remote_copy(
            src_ref=src, dst_ref=dst,
            send_sem=send_sem, recv_sem=recv_sem.at[names.index(name)],
            device_id=device, device_id_type=MESH,
        ).start()

    def settle(sem, size):
        view = blank.at[pl.ds(0, size // (2 * BLK)), :]
        pltpu.make_async_copy(view, view, sem).wait()

    def wait(name):
        settle(recv_sem.at[names.index(name)], bytes_of[name])

    pair = c + 1 - 2 * lax.rem(c, 2)
    across = lax.rem(c + 2, cols)
    far = lax.rem(pair + 2, cols)
    targets = [pair, across, far]

    own = qbuf.shape[1]
    key_count = mask.shape[1]
    attended = []
    home = lax.div(c * own, BLK)
    first = lax.broadcasted_iota(jnp.int32, (BLK, 2 * own), 1) < own

    def visible(slot, j):
        block = home if slot < 2 else 1 - home
        return jnp.where(block == 0, mask[0:1, j : j + 1], mask[1:2, j : j + 1])

    def attend(near, late):
        pair_rows = [qbuf[near], qbuf[late]]
        seen = jnp.concatenate(
            [jnp.where(first, visible(near, j), visible(late, j)) for j in range(key_count)], axis=0
        )
        for h in range(HEADS):
            lanes = slice(h * HD, (h + 1) * HD)
            key_rows = kv[:, 0, :, lanes].reshape(-1, HD)
            value_rows = kv[:, 1, :, lanes].reshape(-1, HD)
            query_rows = jnp.concatenate([rows[:, lanes] for rows in pair_rows], axis=0)
            scores = lax.dot_general(
                key_rows, query_rows, (((1,), (1,)), ((), ())), preferred_element_type=jnp.float32
            )
            scores = jnp.where(seen > 0, scores * score_scale, -jnp.inf)
            tile_max = jnp.max(scores, axis=0, keepdims=True)
            weights = jnp.exp(scores - tile_max)
            tile_total = jnp.sum(weights, axis=0, keepdims=True)
            tile_sum = lax.dot_general(
                weights.astype(jnp.bfloat16), value_rows, (((0,), (0,)), ((), ())),
                preferred_element_type=jnp.float32,
            )
            for i, slot in enumerate((near, late)):
                part = slice(i * own, (i + 1) * own)
                ssend[slot, h : h + 1, 0:own] = tile_max[:, part]
                ssend[slot, HEADS + h : HEADS + h + 1, 0:own] = tile_total[:, part]
                if slot == 0:
                    osum[:, lanes] = tile_sum[part]
                else:
                    psend[slot - 1, :, lanes] = tile_sum[part].astype(jnp.bfloat16)
        for slot in (near, late):
            if slot > 0:
                send(ssend.at[slot], srecv.at[slot - 1], {"col": targets[slot - 1]}, "s")
                send(psend.at[slot - 1], precv.at[slot - 1], {"col": targets[slot - 1]}, "p")

    def prepare():
        wait("s")
        stats = [ssend[0]] + [srecv[t] for t in range(cols - 1)]
        maxes = [s[0:HEADS, :] for s in stats]
        totals = [s[HEADS : 2 * HEADS, :] for s in stats]
        row_max = functools.reduce(jnp.maximum, maxes)
        factors = [jnp.exp(m - row_max) for m in maxes]
        denom = functools.reduce(jnp.add, [t * f for t, f in zip(totals, factors)])
        pad = [jnp.zeros((8 - HEADS, denom.shape[1]), jnp.float32)]
        table = jnp.concatenate([x for f in factors for x in [f / denom] + pad], axis=0)
        fill = jnp.zeros((table.shape[1] - table.shape[0], table.shape[1]), jnp.float32)
        table = jnp.concatenate([table, fill], axis=0).T[0:own]
        for t in range(cols):
            for h in range(HEADS):
                column = table[:, 8 * t + h : 8 * t + h + 1]
                spread_scale[t, h] = jnp.broadcast_to(column, (own, HD))
        for h in range(HEADS):
            lanes = slice(h * HD, (h + 1) * HD)
            osum[:, lanes] = osum[:, lanes] * spread_scale[0, h]
        loads[5].wait()

    def merge():
        wait("p")
        heads = []
        for h in range(HEADS):
            lanes = slice(h * HD, (h + 1) * HD)
            mixed = osum[:, lanes]
            for t in range(1, cols):
                mixed += precv[t - 1, :, lanes].astype(jnp.float32) * spread_scale[t, h]
            heads.append(mixed)
        attended.append(jnp.concatenate(heads, axis=1).astype(jnp.bfloat16))

    width = cols * 2 * wt.shape[3]

    def project(row):
        columns = pl.ds(pl.multiple_of(row * width, BLK), width)
        projected = lax.dot_general(
            attended[0], wt[row].reshape(width, HEADS * HD), (((1,), (1,)), ((), ())),
            preferred_element_type=jnp.float32,
        )
        total = projected + res[:, columns].astype(jnp.float32)
        out_ref[:, columns] = total.astype(jnp.bfloat16)

    loads[3].wait()
    send(wt.at[r, c, g], wt.at[r, c, g], {"col": across}, "across")
    send(wt.at[r, c, g], wt.at[r, c, g], {"col": pair}, "pair")
    loads[0].wait()
    send(qbuf.at[0], qbuf.at[3], {"col": far}, "q_far")
    send(qbuf.at[0], qbuf.at[2], {"col": across}, "q_across")
    send(qbuf.at[0], qbuf.at[1], {"col": pair}, "q_pair")
    loads[1].wait()
    loads[2].wait()
    send(kv.at[r], kv.at[r], chip, "kv_chip")
    send(kv.at[r], kv.at[r], core, "kv_core")
    send(wt.at[r, c], wt.at[r, c], core, "core_r")
    send(wt.at[r, c, g], wt.at[r, c, g], chip, "own_x")
    wait("kv_chip")
    send(kv.at[r_chip], kv.at[r_chip], core, "kv_core")
    wait("pair")
    send(wt.at[r, pair, g], wt.at[r, pair, g], video, "pair_y")
    send(wt.at[r, pair, g], wt.at[r, pair, g], chip, "pair_x")
    send(wt.at[r, pair, g], wt.at[r, pair, g], core, "core_r")
    wait("across")
    send(wt.at[r, across, g], wt.at[r, across, g], {"col": pair}, "far")
    send(wt.at[r, across, g], wt.at[r, across, g], chip, "across_x")
    send(wt.at[r, across, g], wt.at[r, across, g], video, "across_y")
    send(wt.at[r, across, g], wt.at[r, across, g], core, "core_r")
    wait("own_x")
    send(wt.at[r_chip, c, g], wt.at[r_chip, c, g], core, "core_x")
    send(wt.at[r_chip, c, g], wt.at[r_chip, c, g], video, "own_y")
    wait("q_far")
    wait("q_across")
    wait("kv_core")
    loads[4].wait()
    attend(2, 3)
    wait("pair_y")
    send(wt.at[r, pair, other], wt.at[r, pair, other], core, "core_r")
    send(wt.at[r, pair, other], wt.at[r, pair, other], chip, "pair_d")
    wait("q_pair")
    attend(1, 0)
    wait("far")
    send(wt.at[r, far, g], wt.at[r, far, g], video, "far_y")
    send(wt.at[r, far, g], wt.at[r, far, g], diagonal, "far_d")
    send(wt.at[r, far, g], wt.at[r, far, g], chip, "far_x")
    send(wt.at[r, far, g], wt.at[r, far, g], core, "core_r")
    wait("across_x")
    send(wt.at[r_chip, across, g], wt.at[r_chip, across, g], core, "core_x")
    send(wt.at[r_chip, across, g], wt.at[r_chip, across, g], video, "across_d")
    wait("across_y")
    send(wt.at[r, across, other], wt.at[r, across, other], core, "core_r")
    wait("own_y")
    send(wt.at[r_chip, c, other], wt.at[r_chip, c, other], core, "core_x")
    wait("pair_x")
    send(wt.at[r_chip, pair, g], wt.at[r_chip, pair, g], core, "core_x")
    wait("pair_d")
    send(wt.at[r_chip, pair, other], wt.at[r_chip, pair, other], core, "core_x")
    wait("far_y")
    send(wt.at[r, far, other], wt.at[r, far, other], core, "core_r")
    prepare()
    merge()
    project(r)
    wait("far_x")
    send(wt.at[r_chip, far, g], wt.at[r_chip, far, g], core, "core_x")
    wait("far_d")
    send(wt.at[r_chip, far, other], wt.at[r_chip, far, other], core, "core_x")
    wait("across_d")
    send(wt.at[r_chip, across, other], wt.at[r_chip, across, other], core, "core_x")
    project(r_chip)
    wait("core_r")
    project(r_core)
    wait("core_x")
    project(r_both)
    assert len(names) == slots, len(names)
    settle(send_sem, bytes_of[""])


def fused(queries, keys, values, block_mask, out_weight, residual):
    rows, cols = lax.axis_size("row"), lax.axis_size("col")
    own, width = queries.shape
    depth, part = out_weight.shape
    slots = 23
    any_space = pl.BlockSpec(memory_space=pl.ANY)
    return pl.pallas_call(
        functools.partial(fused_kernel, slots),
        out_shape=pltpu.VMEM((own, residual.shape[1]), jnp.bfloat16),
        in_specs=[any_space] * 6,
        out_specs=pl.BlockSpec(memory_space=pltpu.VMEM),
        scratch_shapes=[
            pltpu.VMEM((cols, own, width), jnp.bfloat16),
            pltpu.VMEM((rows, 2, own, width), jnp.bfloat16),
            pltpu.VMEM((rows, cols, 2, part // 2, depth), jnp.bfloat16),
            pltpu.VMEM(block_mask.shape, jnp.int32),
            pltpu.VMEM((cols - 1, own, width), jnp.bfloat16),
            pltpu.VMEM((cols - 1, own, width), jnp.bfloat16),
            pltpu.VMEM((cols, 8, BLK), jnp.float32),
            pltpu.VMEM((cols - 1, 8, BLK), jnp.float32),
            pltpu.VMEM((own, width), jnp.float32),
            pltpu.VMEM((cols, HEADS, own, HD), jnp.float32),
            pltpu.VMEM(residual.shape, jnp.bfloat16),
            pltpu.VMEM((rows * cols * 2 * part * depth // BLK, BLK), jnp.bfloat16),
            pltpu.SemaphoreType.DMA((6,)),
            pltpu.SemaphoreType.DMA,
            pltpu.SemaphoreType.DMA((slots,)),
        ],
        compiler_params=pltpu.CompilerParams(collective_id=0, has_side_effects=True),
    )(queries, keys, values, block_mask, out_weight.T.reshape(2, part // 2, depth), residual)


def kernel_fits(mesh):
    return mesh.shape["groups"] == 2 and mesh.shape["row"] == 4 and mesh.shape["col"] == 4


def solution(mesh):
    body = fused if kernel_fits(mesh) else local
    placed = (
        P(("groups", "row", "col"), None),
        P(("groups", "col", "row"), None),
        P(("groups", "col", "row"), None),
        P(("groups", "row"), "col"),
        P(None, ("row", "col")),
        P(("groups", "row", "col"), None),
    )
    return jax.shard_map(
        body,
        mesh=mesh,
        in_specs=placed,
        out_specs=P(("groups", "row", "col"), None),
        check_vma=False,
    )
```
